256 devices in a mesh: group: 16 (over x, y), member: 16 (over z, core).
Axes of the slice: x: 4, y: 4, z: 8, core: 2. Of those that a mesh axis runs over, the one named last changes fastest.
Arguments:
- embeddings: bfloat16 [24576, 4096], P(('group', 'member'))
- cluster_ids: int32 [24576], P(('group', 'member')), may hold values from 0 to 31, as said below
- order_index: int32 [24576], P(('group', 'member')), may hold values from 0 to 24575, each once
Outputs:
- best_similarity: float32 [24576], P(('group', 'member'))
The draws below stay inside these ranges and needn't reach their ends.
Inputs may be any that keep to these rules, and one draw needn't show every extreme that they name: `cluster_ids`: among the documents of one device, at most 12 have a cluster of any one group index g (cluster // 2 == g), and on every device some group index has exactly 12.
All inputs are finite; a program needn't handle non-finite values.
Results may differ from the reference program's by a relative error of at most 0.0004.
Values may be sent and summed in bfloat16 or wider, within the bound.
A program may use at most 128 MiB of HBM per device.

```python
import jax
import jax.numpy as jnp
from jax import lax

D = 4096
ROW_DEV = 96
CL_GROUP = 2
GROUPS = 16
DEVICE_LIMIT = 12
CLUSTERS = 32
ROWS = 24576


def assign_clusters(key):
    folded = jax.random.fold_in(key, 11)
    keys = jax.random.split(folded, 8)
    device_total = ROWS // ROW_DEV
    position_count = GROUPS * DEVICE_LIMIT
    preferred_choice = jax.random.randint(keys[0], (device_total,), 0, GROUPS)
    spread_jitter = jax.random.randint(keys[1], (device_total, position_count), 0, 4096)
    position_index = jnp.arange(position_count, dtype=jnp.int32)
    extra_credit = jnp.where(position_index[None, :] // DEVICE_LIMIT == preferred_choice[:, None], 2 ** 28, 0)
    rating_value = spread_jitter * position_count + position_index[None, :] + extra_credit
    picked_score, chosen = lax.top_k(rating_value, ROW_DEV)
    shuffle_keys = jax.random.split(keys[2], device_total)
    shuffled = jax.vmap(jax.random.permutation)(shuffle_keys, chosen)
    target_group = shuffled // DEVICE_LIMIT
    first_factor = jax.random.randint(keys[3], (device_total, ROW_DEV), 0, CL_GROUP)
    second_factor = jax.random.randint(keys[4], (device_total, ROW_DEV), 1, CL_GROUP + 1)
    within = first_factor * second_factor // CL_GROUP
    cluster_grid = target_group * CL_GROUP + within
    flagged = jax.random.randint(keys[5], (device_total, ROW_DEV), 0, 10) < 2
    offsets = jax.random.randint(keys[6], (device_total, ROW_DEV, 8), 1, device_total)
    partner = (jnp.arange(device_total, dtype=jnp.int32)[:, None, None] + offsets) % device_total
    candidate_group = target_group[partner]
    candidate_free = jnp.logical_not(flagged[partner])
    candidate_ok = (candidate_group == target_group[:, :, None, None]) & candidate_free
    pool_size = 8 * ROW_DEV
    pick_noise = jax.random.randint(keys[7], (device_total, ROW_DEV, 8, ROW_DEV), 0, 2 ** 19)
    pool_index = jnp.arange(pool_size, dtype=jnp.int32).reshape(8, ROW_DEV)
    candidate_score = jnp.where(candidate_ok, pick_noise * pool_size + pool_index[None, None, :, :], -1)
    candidate_score = candidate_score.reshape(device_total, ROW_DEV, pool_size)
    top_score, top_position = lax.top_k(candidate_score, 1)
    found = top_score[:, :, 0] >= 0
    duplicate = flagged & found
    position = top_position[:, :, 0]
    source_slot = position // ROW_DEV
    source_local = position % ROW_DEV
    source_device = jnp.take_along_axis(partner, source_slot[:, :, None], axis=2)[:, :, 0]
    source = (source_device * ROW_DEV + source_local).reshape(-1).astype(jnp.int32)
    flat_clusters = cluster_grid.reshape(-1)
    duplicate = duplicate.reshape(-1)
    clusters = jnp.where(duplicate, flat_clusters[source], flat_clusters)
    return (clusters.astype(jnp.int32), duplicate, source)


def draw_cluster_ids(key, part):
    clusters, duplicate, source = assign_clusters(key)
    return clusters


def draw_embeddings(key, part):
    clusters, duplicate, source = assign_clusters(key)
    folded = jax.random.fold_in(key, 23)
    keys = jax.random.split(folded, 6)
    centroids = jax.random.normal(keys[0], (CLUSTERS, D), jnp.float32)
    amount = jax.random.uniform(keys[4], (ROWS, 1), jnp.float32, 0.1, 0.7)
    noise = jax.random.normal(keys[2], (ROWS, D), jnp.float32)
    copy_noise = jax.random.normal(keys[5], (ROWS, D), jnp.float32)
    base = centroids[clusters] + noise
    copied = base[source] + amount * copy_noise
    values = jnp.where(duplicate[:, None], copied, base)
    return values.astype(jnp.bfloat16)


def setup_inputs(seed: int = 0) -> dict:
    key_list = jax.random.split(jax.random.key(seed), 4)
    return {
        "embeddings": draw_embeddings(jax.random.fold_in(key_list[3], 71), 0),
        "cluster_ids": draw_cluster_ids(jax.random.fold_in(key_list[3], 71), 0),
        "order_index": jax.random.permutation(key_list[2], ROWS).astype(jnp.int32),
    }


def normalize(embeddings):
    values = embeddings.astype(jnp.float32)
    total = lax.optimization_barrier(jnp.sum(values * values, axis=1, keepdims=True)) + values.shape[1] * 1e-06
    return (values * lax.rsqrt(total)).astype(jnp.bfloat16)

def reference(embeddings, cluster_ids, order_index):
    unit_rows = normalize(embeddings).astype(jnp.float32)
    owner_group = cluster_ids // CL_GROUP
    position_count = ROWS // ROW_DEV * DEVICE_LIMIT

    def per_group(group_number):
        member_rows = jnp.argsort((owner_group != group_number).astype(jnp.int32), stable=True)[:position_count].astype(jnp.int32)
        valid = owner_group[member_rows] == group_number
        block = unit_rows[member_rows]
        block_cluster = jnp.where(valid, cluster_ids[member_rows], -1)
        block_order = order_index[member_rows]
        cosine = jnp.dot(block, block.T, preferred_element_type=jnp.float32, precision=lax.Precision.HIGHEST)
        earlier = (block_cluster[:, None] == block_cluster[None, :]) & (block_cluster[:, None] >= 0)
        earlier = earlier & (block_order[None, :] < block_order[:, None])
        result = lax.optimization_barrier(jnp.max(jnp.where(earlier, cosine, -1.0), axis=1))
        return (member_rows, jnp.where(valid, result, -2.0))
    indices, results = lax.map(per_group, jnp.arange(GROUPS, dtype=jnp.int32))
    base = jnp.full((ROWS,), -2.0, dtype=jnp.float32)
    return base.at[indices.reshape(-1)].max(results.reshape(-1))
```

```python
import functools

import jax
import jax.numpy as jnp
from jax import lax
from jax.experimental import pallas as pl
from jax.experimental.pallas import tpu as pltpu
from jax.sharding import PartitionSpec as P

MESH = pl.DeviceIdType.MESH

NX, NY, NZ = 4, 4, 8
DOCS = 96
CAP = 12
CHUNK = 2 * CAP
SLOTS = NZ * CHUNK
D = 4096
META = 128
W = D + META

XM, XP, X2, OWN, YM, YP, Y2 = range(7)
ORDER = (0, 1, 7, 2, 6, 3, 5, 4)


def nt_dot(a, b, **kw):
    return lax.dot_general(
        a, b, (((1,), (1,)), ((), ())), preferred_element_type=jnp.float32, **kw
    )


def kernel(
    emb_ref,
    ids_ref,
    ord_ref,
    out_ref,
    units,
    mrows,
    outb,
    buf,
    best,
    part,
    ans,
    fin,
    sib_send,
    sib_recv,
    z_send,
    send,
    recv,
    p_send,
    p_recv,
    a_send,
    a_recv,
):
    gi = lax.axis_index("group")
    mi = lax.axis_index("member")
    x, y = gi // NY, lax.rem(gi, NY)
    z, c = mi // 2, lax.rem(mi, 2)

    def at_x(step):
        return (lax.rem(x + step + NX, NX) * NY + y, mi)

    def at_y(step):
        return (x * NY + lax.rem(y + step + NY, NY), mi)

    def at_z(step):
        return (gi, lax.rem(z + step + NZ, NZ) * 2 + c)

    sibling = (gi, z * 2 + 1 - c)

    peers = [sibling, at_x(1), at_x(-1), at_y(1), at_y(-1), at_y(2)]
    peers += [at_z(s) for s in range(1, NZ)]
    barrier = pltpu.get_barrier_semaphore()
    for peer in peers:
        pl.semaphore_signal(barrier, inc=1, device_id=peer, device_id_type=MESH)

    @pl.loop(0, DOCS // 16)
    def _(i):
        rows = pl.ds(pl.multiple_of(i * 16, 16), 16)
        values = emb_ref[rows, :].astype(jnp.float32)
        total = jnp.sum(values * values, axis=1, keepdims=True) + D * 1e-06
        units[0, rows, :] = (values * lax.rsqrt(total)).astype(jnp.bfloat16)

    ids = ids_ref[...]
    order = ord_ref[...]
    target = ids // 2
    hit = lax.broadcasted_iota(jnp.int32, (16, DOCS), 0) == target
    hit_f = hit.astype(jnp.float32)
    tri = lax.broadcasted_iota(jnp.int32, (DOCS, DOCS), 0) < lax.broadcasted_iota(
        jnp.int32, (DOCS, DOCS), 1
    )
    count = jnp.dot(
        hit_f.astype(jnp.bfloat16), tri.astype(jnp.bfloat16), preferred_element_type=jnp.float32
    )
    rank = jnp.sum(hit_f * count, axis=0, keepdims=True).astype(jnp.int32)
    offset = lax.rem(target // 2 - z + NZ, NZ)
    core = lax.rem(target, 2)
    inner = c * CAP + rank
    slot = offset * CHUNK + inner
    to_core0 = jnp.where(core == 0, slot, -1).astype(jnp.float32)
    to_core1 = jnp.where(core == 1, slot, -1).astype(jnp.float32)
    high = order // 256
    low = order - high * 256
    row_id = lax.broadcasted_iota(jnp.int32, (8, DOCS), 0)
    packed = jnp.where(row_id == 0, to_core0, 0.0)
    packed = jnp.where(row_id == 1, to_core1, packed)
    packed = jnp.where(row_id == 2, (ids + 1).astype(jnp.float32), packed)
    packed = jnp.where(row_id == 3, high.astype(jnp.float32), packed)
    packed = jnp.where(row_id == 4, low.astype(jnp.float32), packed)
    mrows[0, :, :DOCS] = packed
    mrows[0, :, DOCS:] = jnp.zeros((8, 128 - DOCS), jnp.float32)

    pl.semaphore_wait(barrier, len(peers))

    waits = []

    def push(src, dst, ssem, rsem, device):
        copy = pltpu.make_async_remote_copy(
            src_ref=src, dst_ref=dst, send_sem=ssem, recv_sem=rsem,
            device_id=device, device_id_type=MESH,
        )
        copy.start()
        waits.append(copy)
        return copy

    meta_copy = push(mrows.at[0], mrows.at[1], sib_send.at[0], sib_recv.at[0], sibling)
    unit_copy = push(units.at[0], units.at[1], sib_send.at[1], sib_recv.at[1], sibling)

    slot_iota = lax.broadcasted_iota(jnp.int32, (SLOTS, DOCS), 0).astype(jnp.float32)

    def table_of(which):
        rows = mrows[which]
        mine = jnp.where(c == 0, rows[0:1, :DOCS], rows[1:2, :DOCS])
        table = (slot_iota == mine).astype(jnp.bfloat16)
        lanes = lax.broadcasted_iota(jnp.int32, (META, DOCS), 0)
        cols = jnp.where(lanes == 0, rows[2:3, :DOCS], 0.0)
        cols = jnp.where(lanes == 1, rows[3:4, :DOCS], cols)
        cols = jnp.where(lanes == 2, rows[4:5, :DOCS], cols)
        return table, nt_dot(table, cols.astype(jnp.bfloat16))

    table_a, meta_a = table_of(0)
    meta_copy.wait_recv()
    table_b, meta_b = table_of(1)
    unit_copy.wait_recv()

    def place(values, columns):
        values = values.reshape(NZ, CHUNK, values.shape[-1]).astype(jnp.bfloat16)
        buf[OWN, 0, :, columns] = values[0]
        outb[:, :, columns] = values[1:]

    place(meta_a + meta_b, pl.ds(D, META))

    @pl.loop(0, D // 512)
    def _(i):
        columns = pl.ds(pl.multiple_of(i * 512, 512), 512)
        rows = jnp.dot(table_a, units[0, :, columns], preferred_element_type=jnp.float32)
        rows += jnp.dot(table_b, units[1, :, columns], preferred_element_type=jnp.float32)
        place(rows, columns)

    own_copies = {}
    for k in ORDER[1:]:
        own_copies[k] = push(outb.at[k - 1], buf.at[OWN, k], z_send.at[k], recv.at[OWN, k], at_z(k))

    arrive = {}

    def forward(src, entry, k, device):
        arrive[entry, k] = push(
            buf.at[src, k], buf.at[entry, k], send.at[entry, k], recv.at[entry, k], device
        )

    done = set()

    def arrived(entry, k):
        if (entry, k) not in done:
            done.add((entry, k))
            arrive[entry, k].wait_recv()

    def relay(i):
        k = ORDER[i]
        if i % 2 == 0:
            arrived(XM, k)
            forward(XM, X2, k, at_x(1))
            arrived(YM, k)
            forward(YM, Y2, k, at_y(1))
        else:
            arrived(XP, k)
            forward(XP, X2, k, at_x(-1))
            arrived(YP, k)
            forward(YP, Y2, k, at_y(-1))

    for i, k in enumerate(ORDER):
        if k:
            own_copies[k].wait_recv()
        forward(OWN, XM, k, at_x(1))
        forward(OWN, XP, k, at_x(-1))
        forward(OWN, YM, k, at_y(1))
        forward(OWN, YP, k, at_y(-1))
        if i:
            relay(i - 1)
    relay(NZ - 1)
    for k in ORDER:
        for entry in (XM, XP, YM, YP, X2, Y2):
            arrived(entry, k)

    best[...] = jnp.full(best.shape, -1.0, jnp.float32)
    pick_row = lax.broadcasted_iota(jnp.int32, (8, META), 0)
    pick_lane = lax.broadcasted_iota(jnp.int32, (8, META), 1)
    pick = jnp.where((pick_row == 0) & (pick_lane == 0), 1.0, 0.0)
    pick = jnp.where((pick_row == 1) & (pick_lane == 1), 256.0, pick)
    pick = jnp.where((pick_row == 1) & (pick_lane == 2), 1.0, pick).astype(jnp.bfloat16)

    @pl.loop(0, 16)
    def _(i):
        r, col = i // 4, OWN + lax.rem(i, 4)
        rows = buf[r, :, :, :D].reshape(SLOTS, D)
        columns = buf[col, :, :, :D].reshape(SLOTS, D)
        cosine = nt_dot(rows, columns)
        rmeta = buf[r, :, :, D:].reshape(SLOTS, META).astype(jnp.float32)
        cmeta = nt_dot(pick, buf[col, :, :, D:].reshape(SLOTS, META))
        rank_r = rmeta[:, 1:2] * 256.0 + rmeta[:, 2:3]
        keep = (rmeta[:, 0:1] == cmeta[0:1, :]) & (rank_r < cmeta[1:2, :])
        masked = jnp.where(keep, cosine, -1.0).reshape(SLOTS // 8, 8, SLOTS)
        j = col - OWN
        best[j, :, :SLOTS] = jnp.maximum(best[j, :, :SLOTS], jnp.max(masked, axis=0))

    p_copies = []
    for n, (entry, step) in enumerate(((YM, -1), (YP, 1), (Y2, 2))):
        p_copies.append(
            push(best.at[entry - OWN], part.at[n], p_send.at[n], p_recv.at[n], at_y(step))
        )
    for copy in p_copies:
        copy.wait_recv()
    total = jnp.maximum(
        jnp.maximum(best[0], part[0]), jnp.maximum(part[1], part[2])
    )
    total = jnp.max(total, axis=0, keepdims=True)
    ans[0] = jnp.broadcast_to(total, (8, 256))
    a_copies = []
    for k in range(1, NZ):
        a_copies.append(push(ans.at[0], ans.at[k], a_send.at[k], a_recv.at[k], at_z(-k)))
    for copy in a_copies:
        copy.wait_recv()
    fin[0] = jnp.zeros((8, 128), jnp.float32)
    for k in range(NZ):
        fin[0, k : k + 1, :CHUNK] = ans[k, 0:1, k * CHUNK : (k + 1) * CHUNK]
    fin_copy = push(fin.at[0], fin.at[1], sib_send.at[2], sib_recv.at[2], sibling)
    spot = (lax.broadcasted_iota(jnp.int32, (128, DOCS), 0) == inner).astype(jnp.float32)
    offs = lax.broadcasted_iota(jnp.int32, (8, DOCS), 0) == offset
    fin_copy.wait_recv()
    picked = jnp.zeros((8, DOCS), jnp.float32)
    for n in range(2):
        values = jnp.dot(
            fin[n], spot, preferred_element_type=jnp.float32, precision=lax.Precision.HIGHEST
        )
        at_core = jnp.where(core == (c if n == 0 else 1 - c), 1, 0)
        picked += jnp.where(offs & (at_core == 1), values, 0.0)
    out_ref[...] = jnp.sum(picked, axis=0, keepdims=True)
    for copy in waits:
        copy.wait_send()


def local(embeddings, cluster_ids, order_index):
    dma = pltpu.SemaphoreType.DMA
    vmem = pl.BlockSpec(memory_space=pltpu.VMEM)
    result = pl.pallas_call(
        kernel,
        out_shape=jax.ShapeDtypeStruct((1, DOCS), jnp.float32),
        in_specs=[vmem] * 3,
        out_specs=vmem,
        scratch_shapes=[
            pltpu.VMEM((2, DOCS, D), jnp.bfloat16),
            pltpu.VMEM((2, 8, 128), jnp.float32),
            pltpu.VMEM((NZ - 1, CHUNK, W), jnp.bfloat16),
            pltpu.VMEM((7, NZ, CHUNK, W), jnp.bfloat16),
            pltpu.VMEM((4, 8, 256), jnp.float32),
            pltpu.VMEM((3, 8, 256), jnp.float32),
            pltpu.VMEM((NZ, 8, 256), jnp.float32),
            pltpu.VMEM((2, 8, 128), jnp.float32),
            dma((3,)),
            dma((3,)),
            dma((NZ,)),
            dma((7, NZ)),
            dma((7, NZ)),
            dma((3,)),
            dma((3,)),
            dma((NZ,)),
            dma((NZ,)),
        ],
        compiler_params=pltpu.CompilerParams(
            collective_id=0, has_side_effects=True, vmem_limit_bytes=48 * 1024 * 1024
        ),
    )(embeddings, cluster_ids.reshape(1, DOCS), order_index.reshape(1, DOCS))
    return result.reshape(DOCS)


def solution(mesh):
    placed = (P(("group", "member"), None), P(("group", "member")), P(("group", "member")))
    return jax.shard_map(
        local, mesh=mesh, in_specs=placed, out_specs=P(("group", "member")), check_vma=False
    )
```

```python
import jax
import jax.numpy as jnp
from jax import lax
from jax.experimental import pallas as pl
from jax.experimental.pallas import tpu as pltpu
from jax.sharding import PartitionSpec as P

MESH = pl.DeviceIdType.MESH

NX, NY, NZ = 4, 4, 8
DOCS = 96
CAP = 12
CHUNK = 2 * CAP
SLOTS = NZ * CHUNK
D = 4096
META = 128
WIDTHS = (512,) * 8
STARTS = tuple(sum(WIDTHS[:p]) for p in range(len(WIDTHS)))
PARTS = len(WIDTHS)

OWN, XY, X1, X2, Y1, Y2 = range(6)
BLOCKS = 6
RETURNS = (X1, Y1, XY, X2, Y2)


def nt_dot(a, b):
    return lax.dot_general(
        a, b, (((1,), (1,)), ((), ())), preferred_element_type=jnp.float32
    )


def kernel(*refs):
    emb_hbm, ids_hbm, ord_hbm, out_ref, emb, ids_ref, ord_ref = refs[:7]
    downs, mrows, best, part, ans, fin, acc_own, acc_xy, units = refs[7:16]
    outb = refs[16 : 16 + PARTS]
    buf = refs[16 + PARTS : 16 + 2 * PARTS]
    (
        in_sem, sib_send, sib_recv, z_send, z_recv, send, recv, p_send, p_recv, a_send, a_recv,
    ) = refs[16 + 2 * PARTS :]

    gi = lax.axis_index("group")
    mi = lax.axis_index("member")
    x, y = gi // NY, lax.rem(gi, NY)
    z, c = mi // 2, lax.rem(mi, 2)
    sign = 1 - 2 * c

    def at(dx, dy):
        return (
            lax.rem(x + sign * dx + NX, NX) * NY + lax.rem(y + sign * dy + NY, NY),
            mi,
        )

    def at_z(step):
        return (gi, lax.rem(z + step + NZ, NZ) * 2 + c)

    sibling = (gi, z * 2 + 1 - c)
    back = {X1: at(-1, 0), Y1: at(0, -1), XY: at(-1, -1), X2: at(-2, 0), Y2: at(0, -2)}

    loads = [
        pltpu.make_async_copy(ids_hbm, ids_ref, in_sem.at[0]),
        pltpu.make_async_copy(ord_hbm, ord_ref, in_sem.at[1]),
        pltpu.make_async_copy(emb_hbm, emb, in_sem.at[2]),
    ]
    for load in loads:
        load.start()

    peers = [sibling, at(1, 0), at(0, 1), at(1, 1), at(-1, 0), at(0, -1), at(-1, -1)]
    peers += [at(2, 0), at(0, 2)] + [at_z(s) for s in range(1, NZ)]
    barrier = pltpu.get_barrier_semaphore()
    for peer in peers:
        pl.semaphore_signal(barrier, inc=1, device_id=peer, device_id_type=MESH)

    loads[0].wait()
    loads[1].wait()
    ids = ids_ref[...]
    order = ord_ref[...]
    target = ids // 2
    hit = lax.broadcasted_iota(jnp.int32, (16, DOCS), 0) == target
    hit_f = hit.astype(jnp.float32)
    tri = lax.broadcasted_iota(jnp.int32, (DOCS, DOCS), 0) < lax.broadcasted_iota(
        jnp.int32, (DOCS, DOCS), 1
    )
    count = jnp.dot(
        hit_f.astype(jnp.bfloat16), tri.astype(jnp.bfloat16), preferred_element_type=jnp.float32
    )
    rank = jnp.sum(hit_f * count, axis=0, keepdims=True).astype(jnp.int32)
    offset = lax.rem(target // 2 - z + NZ, NZ)
    core = lax.rem(target, 2)
    inner = c * CAP + rank
    slot = offset * CHUNK + inner
    to_core0 = jnp.where(core == 0, slot, -1).astype(jnp.float32)
    to_core1 = jnp.where(core == 1, slot, -1).astype(jnp.float32)
    high = order // 256
    low = order - high * 256
    row_id = lax.broadcasted_iota(jnp.int32, (8, DOCS), 0)
    packed = jnp.where(row_id == 0, to_core0, 0.0)
    packed = jnp.where(row_id == 1, to_core1, packed)
    packed = jnp.where(row_id == 2, (ids + 1).astype(jnp.float32), packed)
    packed = jnp.where(row_id == 3, high.astype(jnp.float32), packed)
    packed = jnp.where(row_id == 4, low.astype(jnp.float32), packed)
    mrows[0, :, :DOCS] = packed
    mrows[0, :, DOCS:] = jnp.zeros((8, 128 - DOCS), jnp.float32)

    loads[2].wait()

    @pl.loop(0, DOCS // 16)
    def _(i):
        rows = pl.ds(pl.multiple_of(i * 16, 16), 16)
        values = emb[rows, :].astype(jnp.float32)
        total = jnp.sum(values * values, axis=1, keepdims=True) + D * 1e-06
        units[0, rows, :] = (values * lax.rsqrt(total)).astype(jnp.bfloat16)

    pl.semaphore_wait(barrier, len(peers))

    sent = []

    def push(src, dst, ssem, rsem, device):
        copy = pltpu.make_async_remote_copy(
            src_ref=src, dst_ref=dst, send_sem=ssem, recv_sem=rsem,
            device_id=device, device_id_type=MESH,
        )
        copy.start()
        sent.append(copy)
        return copy

    meta_copy = push(
        mrows.at[0], mrows.at[1], sib_send.at[PARTS], sib_recv.at[PARTS], sibling
    )
    unit_copies = []
    for p in range(PARTS):
        columns = pl.ds(STARTS[p], WIDTHS[p])
        unit_copies.append(
            push(
                units.at[0, :, columns], units.at[1, :, columns],
                sib_send.at[p], sib_recv.at[p], sibling,
            )
        )

    slot_iota = lax.broadcasted_iota(jnp.int32, (SLOTS, DOCS), 0).astype(jnp.float32)

    def table_of(which):
        rows = mrows[which]
        mine = jnp.where(c == 0, rows[0:1, :DOCS], rows[1:2, :DOCS])
        table = (slot_iota == mine).astype(jnp.bfloat16)
        lanes = lax.broadcasted_iota(jnp.int32, (META, DOCS), 0)
        cols = jnp.where(lanes == 0, rows[2:3, :DOCS], 0.0)
        cols = jnp.where(lanes == 1, rows[3:4, :DOCS], cols)
        cols = jnp.where(lanes == 2, rows[4:5, :DOCS], cols)
        return table, nt_dot(table, cols.astype(jnp.bfloat16))

    table_a, meta_a = table_of(0)
    meta_copy.wait_recv()
    table_b, meta_b = table_of(1)

    def place(p, values, start):
        width = values.shape[-1]
        values = values.reshape(NZ, CHUNK, width).astype(jnp.bfloat16)
        buf[p][OWN, 0, :, start : start + width] = values[0]
        outb[p][:, :, start : start + width] = values[1:]

    z_copies = {}
    place(0, meta_a + meta_b, WIDTHS[0])
    for p in range(PARTS):
        unit_copies[p].wait_recv()
        columns = pl.ds(STARTS[p], WIDTHS[p])
        rows = jnp.dot(table_a, units[0, :, columns], preferred_element_type=jnp.float32)
        rows += jnp.dot(table_b, units[1, :, columns], preferred_element_type=jnp.float32)
        place(p, rows, 0)
        for k in (1, 7, 2, 6, 3, 5, 4):
            z_copies[p, k] = push(
                outb[p].at[k - 1], buf[p].at[OWN, k], z_send.at[p, k], z_recv.at[p, k], at_z(k)
            )

    copies = {}

    def forward(src, dst, p, device):
        copies[dst, p] = push(
            buf[p].at[src], buf[p].at[dst], send.at[dst, p], recv.at[dst, p], device
        )

    done = set()

    def arrived(block, p):
        if (block, p) not in done:
            done.add((block, p))
            copies[block, p].wait_recv()

    def relay(p):
        arrived(X1, p)
        forward(X1, X2, p, at(1, 0))
        if p % 2 == 0:
            forward(X1, XY, p, at(0, 1))
        arrived(Y1, p)
        forward(Y1, Y2, p, at(0, 1))
        if p % 2 == 1:
            forward(Y1, XY, p, at(1, 0))

    def multiply(p):
        for block in (XY, X2, Y2):
            arrived(block, p)
        w = WIDTHS[p]
        rows = buf[p][OWN, :, :, :w].reshape(SLOTS, w)
        for block in range(BLOCKS):
            acc_own[block] += nt_dot(buf[p][block, :, :, :w].reshape(SLOTS, w), rows)
        for b in range(2):
            columns = buf[p][Y1 + b, :, :, :w].reshape(SLOTS, w)
            for a in range(2):
                acc_xy[a, b] += nt_dot(buf[p][X1 + a, :, :, :w].reshape(SLOTS, w), columns)

    pick_row = lax.broadcasted_iota(jnp.int32, (8, META), 0)
    pick_lane = lax.broadcasted_iota(jnp.int32, (8, META), 1)
    pick = jnp.where((pick_row == 0) & (pick_lane == 0), 1.0, 0.0)
    pick = jnp.where((pick_row == 1) & (pick_lane == 1), 256.0, pick)
    pick = jnp.where((pick_row == 1) & (pick_lane == 2), 1.0, pick).astype(jnp.bfloat16)

    def meta_of(block):
        return buf[0][block, :, :, WIDTHS[0] :].reshape(SLOTS, META)

    def meta_down(block):
        values = meta_of(block).astype(jnp.float32)
        return values[:, 0:1], values[:, 1:2] * 256.0 + values[:, 2:3]

    def meta_across(block):
        values = nt_dot(pick, meta_of(block))
        return values[0:1, :], values[1:2, :]

    def start_sums():
        for block in (XY, X2, Y2):
            arrived(block, 0)
        across = {b: meta_across(b)[0] for b in (OWN, Y1, Y2)}
        for block in range(BLOCKS):
            down = meta_down(block)[0]
            acc_own[block] = jnp.where(down == across[OWN], 0.0, -4.0)
            if block in (X1, X2):
                for b in range(2):
                    acc_xy[block - X1, b] = jnp.where(down == across[Y1 + b], 0.0, -4.0)
        downs[...] = jnp.full(downs.shape, -1.0, jnp.float32)

    for p in range(PARTS):
        for k in (1, 7, 2, 6, 3, 5, 4):
            z_copies[p, k].wait_recv()
        forward(OWN, X1, p, at(1, 0))
        forward(OWN, Y1, p, at(0, 1))
        if p >= 1:
            relay(p - 1)
        if p == 2:
            start_sums()
        if p >= 2:
            multiply(p - 2)
    relay(PARTS - 1)
    multiply(PARTS - 2)
    multiply(PARTS - 1)

    def over_rows(sums, down, across):
        kept = jnp.where(down < across, sums, -1.0)
        return jnp.max(kept.reshape(SLOTS // 8, 8, SLOTS), axis=0)

    def over_columns(sums, down, across):
        return jnp.where(across < down, sums, -1.0)

    across = {b: meta_across(b)[1] for b in (OWN, Y1, Y2)}
    down = {b: meta_down(b)[1] for b in range(BLOCKS)}
    lanes = {b: None for b in range(BLOCKS)}
    rows = {b: None for b in range(BLOCKS)}

    def merge(table, key, value):
        table[key] = value if table[key] is None else jnp.maximum(table[key], value)

    for a in range(2):
        for b in range(2):
            sums = acc_xy[a, b]
            merge(rows, X1 + a, over_columns(sums, down[X1 + a], across[Y1 + b]))
            if (a, b) != (1, 1):
                merge(lanes, Y1 + b, over_rows(sums, down[X1 + a], across[Y1 + b]))
    for block in range(BLOCKS):
        sums = acc_own[block]
        merge(lanes, OWN, over_rows(sums, down[block], across[OWN]))
        if block in (XY, X1, Y1):
            merge(rows, block, over_columns(sums, down[block], across[OWN]))
    for n, block in enumerate((XY, X1, X2, Y1)):
        downs[n, :, :SLOTS] = rows[block]
        narrow = jnp.maximum(downs[n, :, :128], downs[n, :, 128:])
        turned = jnp.max(narrow.T, axis=0, keepdims=True)
        merge(lanes, block, jnp.broadcast_to(turned, (8, SLOTS)))
    for block in range(BLOCKS):
        best[block, :, :SLOTS] = lanes[block]

    p_copies = []
    for n, block in enumerate(RETURNS):
        p_copies.append(push(best.at[block], part.at[n], p_send.at[n], p_recv.at[n], back[block]))
    total = best[OWN]
    for n in range(len(RETURNS)):
        p_copies[n].wait_recv()
        total = jnp.maximum(total, part[n])
    total = jnp.max(total, axis=0, keepdims=True)
    ans[0] = jnp.broadcast_to(total, (8, 256))
    a_copies = []
    for k in range(1, NZ):
        a_copies.append(push(ans.at[0], ans.at[k], a_send.at[k], a_recv.at[k], at_z(-k)))
    for copy in a_copies:
        copy.wait_recv()
    fin[0] = jnp.zeros((8, 128), jnp.float32)
    for k in range(NZ):
        fin[0, k : k + 1, :CHUNK] = ans[k, 0:1, k * CHUNK : (k + 1) * CHUNK]
    fin_copy = push(
        fin.at[0], fin.at[1], sib_send.at[PARTS + 1], sib_recv.at[PARTS + 1], sibling
    )
    spot = (lax.broadcasted_iota(jnp.int32, (128, DOCS), 0) == inner).astype(jnp.float32)
    offs = lax.broadcasted_iota(jnp.int32, (8, DOCS), 0) == offset
    fin_copy.wait_recv()
    picked = jnp.zeros((8, DOCS), jnp.float32)
    for n in range(2):
        values = jnp.dot(
            fin[n], spot, preferred_element_type=jnp.float32, precision=lax.Precision.HIGHEST
        )
        at_core = jnp.where(core == (c if n == 0 else 1 - c), 1, 0)
        picked += jnp.where(offs & (at_core == 1), values, 0.0)
    out_ref[...] = jnp.sum(picked, axis=0, keepdims=True)
    for copy in sent:
        copy.wait_send()


def local(embeddings, cluster_ids, order_index):
    dma = pltpu.SemaphoreType.DMA
    f32, bf16 = jnp.float32, jnp.bfloat16
    widths = [w + (META if p == 0 else 0) for p, w in enumerate(WIDTHS)]
    result = pl.pallas_call(
        kernel,
        out_shape=jax.ShapeDtypeStruct((1, DOCS), jnp.float32),
        in_specs=[pl.BlockSpec(memory_space=pltpu.HBM)] * 3,
        out_specs=pl.BlockSpec(memory_space=pltpu.VMEM),
        scratch_shapes=[
            pltpu.VMEM((DOCS, D), bf16),
            pltpu.VMEM((1, DOCS), jnp.int32),
            pltpu.VMEM((1, DOCS), jnp.int32),
            pltpu.VMEM((4, SLOTS, 256), f32),
            pltpu.VMEM((2, 8, 128), f32),
            pltpu.VMEM((BLOCKS, 8, 256), f32),
            pltpu.VMEM((len(RETURNS), 8, 256), f32),
            pltpu.VMEM((NZ, 8, 256), f32),
            pltpu.VMEM((2, 8, 128), f32),
            pltpu.VMEM((BLOCKS, SLOTS, SLOTS), f32),
            pltpu.VMEM((2, 2, SLOTS, SLOTS), f32),
            pltpu.VMEM((2, DOCS, D), bf16),
        ]
        + [pltpu.VMEM((NZ - 1, CHUNK, w), bf16) for w in widths]
        + [pltpu.VMEM((BLOCKS, NZ, CHUNK, w), bf16) for w in widths]
        + [
            dma((3,)),
            dma((PARTS + 2,)),
            dma((PARTS + 2,)),
            dma((PARTS, NZ)),
            dma((PARTS, NZ)),
            dma((BLOCKS, PARTS)),
            dma((BLOCKS, PARTS)),
            dma((len(RETURNS),)),
            dma((len(RETURNS),)),
            dma((NZ,)),
            dma((NZ,)),
        ],
        compiler_params=pltpu.CompilerParams(
            collective_id=0, has_side_effects=True, vmem_limit_bytes=48 * 1024 * 1024
        ),
    )(embeddings, cluster_ids.reshape(1, DOCS), order_index.reshape(1, DOCS))
    return result.reshape(DOCS)


def solution(mesh):
    placed = (P(("group", "member"), None), P(("group", "member")), P(("group", "member")))
    return jax.shard_map(
        local, mesh=mesh, in_specs=placed, out_specs=P(("group", "member")), check_vma=False
    )
```

```python
import jax
import jax.numpy as jnp
from jax import lax
from jax.experimental import pallas as pl
from jax.experimental.pallas import tpu as pltpu
from jax.sharding import PartitionSpec as P

MESH = pl.DeviceIdType.MESH

NX, NY, NZ = 4, 4, 8
DOCS = 96
CAP = 12
CHUNK = 2 * CAP
SLOTS = NZ * CHUNK
D = 4096
META = 128
W = META + D
WIDTHS = (256,) + (512,) * 7 + (256,)
PARTS = len(WIDTHS)
STARTS = tuple(META + sum(WIDTHS[:p]) for p in range(PARTS))
ENDS = tuple(s + w for s, w in zip(STARTS, WIDTHS))
FAR = (4, 3, 5, 2, 6, 1, 7)
REST = pl.ds(1, NZ - 1)

OWN, XY, X1, X2, Y1, Y2 = range(6)
BLOCKS = 6
RETURNS = (X1, Y1, XY, X2, Y2)


def nt_dot(a, b):
    return lax.dot_general(
        a, b, (((1,), (1,)), ((), ())), preferred_element_type=jnp.float32
    )


def kernel(*refs):
    emb_hbm, ids_hbm, ord_hbm, out_ref, emb, ids_ref, ord_ref = refs[:7]
    downs, mrows, best, part, total_ref, ans, acc_own, acc_xy, units, outb, buf = refs[7:18]
    (
        in_sem, sib_send, sib_recv, z_send, z_recv, send, recv, p_send, p_recv, a_send, a_recv,
        near, far,
    ) = refs[18:]

    gi = lax.axis_index("group")
    mi = lax.axis_index("member")
    x, y = gi // NY, lax.rem(gi, NY)
    z, c = mi // 2, lax.rem(mi, 2)
    sign = 1 - 2 * c

    def at(dx, dy):
        return (
            lax.rem(x + sign * dx + NX, NX) * NY + lax.rem(y + sign * dy + NY, NY),
            mi,
        )

    def at_z(step, core=c):
        return (gi, lax.rem(z + step + NZ, NZ) * 2 + core)

    sibling = at_z(0, 1 - c)
    back = {X1: at(-1, 0), Y1: at(0, -1), XY: at(-1, -1), X2: at(-2, 0), Y2: at(0, -2)}

    loads = [
        pltpu.make_async_copy(ids_hbm, ids_ref, in_sem.at[0]),
        pltpu.make_async_copy(ord_hbm, ord_ref, in_sem.at[1]),
        pltpu.make_async_copy(emb_hbm, emb, in_sem.at[2]),
    ]
    for load in loads:
        load.start()

    peers = [sibling, at(1, 0), at(0, 1), at(-1, 0), at(0, -1), at_z(1), at_z(-1)]
    barrier = pltpu.get_barrier_semaphore()
    for peer in peers:
        pl.semaphore_signal(barrier, inc=1, device_id=peer, device_id_type=MESH)

    loads[0].wait()
    loads[1].wait()
    ids = ids_ref[...]
    order = ord_ref[...]
    target = ids // 2
    hit = lax.broadcasted_iota(jnp.int32, (16, DOCS), 0) == target
    hit_f = hit.astype(jnp.float32)
    tri = lax.broadcasted_iota(jnp.int32, (DOCS, DOCS), 0) < lax.broadcasted_iota(
        jnp.int32, (DOCS, DOCS), 1
    )
    count = jnp.dot(
        hit_f.astype(jnp.bfloat16), tri.astype(jnp.bfloat16), preferred_element_type=jnp.float32
    )
    rank = jnp.sum(hit_f * count, axis=0, keepdims=True).astype(jnp.int32)
    offset = lax.rem(target // 2 - z + NZ, NZ)
    core = lax.rem(target, 2)
    inner = c * CAP + rank
    slot = offset * CHUNK + inner
    to_core0 = jnp.where(core == 0, slot, -1).astype(jnp.float32)
    to_core1 = jnp.where(core == 1, slot, -1).astype(jnp.float32)
    high = order // 256
    low = order - high * 256
    row_id = lax.broadcasted_iota(jnp.int32, (8, DOCS), 0)
    packed = jnp.where(row_id == 0, to_core0, 0.0)
    packed = jnp.where(row_id == 1, to_core1, packed)
    packed = jnp.where(row_id == 2, (ids + 1).astype(jnp.float32), packed)
    packed = jnp.where(row_id == 3, high.astype(jnp.float32), packed)
    packed = jnp.where(row_id == 4, low.astype(jnp.float32), packed)
    mrows[0, :, :DOCS] = packed
    mrows[0, :, DOCS:] = jnp.zeros((8, 128 - DOCS), jnp.float32)

    loads[2].wait()

    @pl.loop(0, DOCS // 16)
    def _(i):
        rows = pl.ds(pl.multiple_of(i * 16, 16), 16)
        values = emb[rows, :].astype(jnp.float32)
        total = jnp.sum(values * values, axis=1, keepdims=True) + D * 1e-06
        units[0, rows, :] = (values * lax.rsqrt(total)).astype(jnp.bfloat16)

    pl.semaphore_wait(barrier, len(peers))

    for step in (1, -1):
        pl.semaphore_signal(near, inc=1, device_id=at_z(step), device_id_type=MESH)

    sent = []

    def push(src, dst, ssem, rsem, device):
        copy = pltpu.make_async_remote_copy(
            src_ref=src, dst_ref=dst, send_sem=ssem, recv_sem=rsem,
            device_id=device, device_id_type=MESH,
        )
        copy.start()
        sent.append(copy)
        return copy

    meta_copy = push(
        mrows.at[0], mrows.at[1], sib_send.at[1], sib_recv.at[1], sibling
    )
    unit_copy = push(units.at[0], units.at[1], sib_send.at[0], sib_recv.at[0], sibling)

    slot_iota = lax.broadcasted_iota(jnp.int32, (SLOTS, DOCS), 0).astype(jnp.float32)

    def table_of(which):
        rows = mrows[which]
        mine = jnp.where(c == 0, rows[0:1, :DOCS], rows[1:2, :DOCS])
        table = (slot_iota == mine).astype(jnp.bfloat16)
        lanes = lax.broadcasted_iota(jnp.int32, (META, DOCS), 0)
        cols = jnp.where(lanes == 0, rows[2:3, :DOCS], 0.0)
        cols = jnp.where(lanes == 1, rows[3:4, :DOCS], cols)
        cols = jnp.where(lanes == 2, rows[4:5, :DOCS], cols)
        return table, nt_dot(table, cols.astype(jnp.bfloat16))

    table_a, meta_a = table_of(0)
    meta_copy.wait_recv()
    table_b, meta_b = table_of(1)

    pl.semaphore_wait(near, 2)
    for step in (2, -2):
        pl.semaphore_signal(far, inc=1, device_id=at_z(step), device_id_type=MESH)

    copies = {}

    def forward(src, dst, p, device):
        if p < 0:
            piece = lambda block: buf.at[block, 0]
        else:
            lo = 0 if p == 0 else STARTS[p]
            columns = pl.ds(lo, ENDS[p] - lo)
            piece = lambda block: buf.at[block, REST, :, columns]
        copies[dst, p] = push(
            piece(src), piece(dst), send.at[dst, p + 1], recv.at[dst, p + 1], device
        )

    unit_copy.wait_recv()
    meta = (meta_a + meta_b).reshape(NZ, CHUNK, META).astype(jnp.bfloat16)
    buf[OWN, 0, :, :META] = meta[0]
    outb[:, :, :META] = meta[1:]
    for p in range(PARTS):
        columns = pl.ds(STARTS[p] - META, WIDTHS[p])
        rows = jnp.dot(
            table_a[:CHUNK], units[0, :, columns], preferred_element_type=jnp.float32
        )
        rows += jnp.dot(
            table_b[:CHUNK], units[1, :, columns], preferred_element_type=jnp.float32
        )
        buf[OWN, 0, :, STARTS[p] : ENDS[p]] = rows.astype(jnp.bfloat16)
    forward(OWN, X1, -1, at(1, 0))
    forward(OWN, Y1, -1, at(0, 1))

    z_copies = {}
    for p in range(PARTS):
        columns = pl.ds(STARTS[p] - META, WIDTHS[p])
        rows = jnp.dot(
            table_a[CHUNK:], units[0, :, columns], preferred_element_type=jnp.float32
        )
        rows += jnp.dot(
            table_b[CHUNK:], units[1, :, columns], preferred_element_type=jnp.float32
        )
        outb[:, :, STARTS[p] : ENDS[p]] = rows.reshape(NZ - 1, CHUNK, WIDTHS[p]).astype(
            jnp.bfloat16
        )
        if p == 0:
            pl.semaphore_wait(far, 2)
        lo = 0 if p == 0 else STARTS[p]
        columns = pl.ds(lo, ENDS[p] - lo)
        for k in FAR:
            z_copies[p, k] = push(
                outb.at[k - 1, :, columns], buf.at[OWN, k, :, columns],
                z_send.at[p, k], z_recv.at[p, k], at_z(k),
            )

    done = set()

    def arrived(block, p):
        if (block, p) not in done:
            done.add((block, p))
            copies[block, p].wait_recv()

    def relay(p):
        arrived(X1, p)
        forward(X1, X2, p, at(1, 0))
        if p % 2 == 0:
            forward(X1, XY, p, at(0, 1))
        arrived(Y1, p)
        forward(Y1, Y2, p, at(0, 1))
        if p % 2 == 1:
            forward(Y1, XY, p, at(1, 0))

    def multiply(p):
        for block in (XY, X2, Y2):
            arrived(block, p)
        columns = pl.ds(STARTS[p], WIDTHS[p])

        def rows_of(block):
            return buf[block, :, :, columns].reshape(SLOTS, WIDTHS[p])

        rows = rows_of(OWN)
        for block in range(BLOCKS):
            acc_own[block] += nt_dot(rows_of(block), rows)
        for b in range(2):
            rows = rows_of(Y1 + b)
            for a in range(2):
                acc_xy[a, b] += nt_dot(rows_of(X1 + a), rows)

    pick_row = lax.broadcasted_iota(jnp.int32, (8, META), 0)
    pick_lane = lax.broadcasted_iota(jnp.int32, (8, META), 1)
    pick = jnp.where((pick_row == 0) & (pick_lane == 0), 1.0, 0.0)
    pick = jnp.where((pick_row == 1) & (pick_lane == 1), 256.0, pick)
    pick = jnp.where((pick_row == 1) & (pick_lane == 2), 1.0, pick).astype(jnp.bfloat16)

    def meta_of(block):
        return buf[block, :, :, :META].reshape(SLOTS, META)

    def meta_down(block):
        values = meta_of(block).astype(jnp.float32)
        return values[:, 0:1], values[:, 1:2] * 256.0 + values[:, 2:3]

    def meta_across(block):
        values = nt_dot(pick, meta_of(block))
        return values[0:1, :], values[1:2, :]

    def start_sums():
        for block in (XY, X2, Y2):
            arrived(block, -1)
            arrived(block, 0)
        across = {b: meta_across(b)[0] for b in (OWN, Y1, Y2)}
        for block in range(BLOCKS):
            down = meta_down(block)[0]
            acc_own[block] = jnp.where(down == across[OWN], 0.0, -4.0)
            if block in (X1, X2):
                for b in range(2):
                    acc_xy[block - X1, b] = jnp.where(down == across[Y1 + b], 0.0, -4.0)
        downs[...] = jnp.full(downs.shape, -1.0, jnp.float32)

    for p in range(PARTS):
        for k in FAR:
            z_copies[p, k].wait_recv()
        forward(OWN, X1, p, at(1, 0))
        forward(OWN, Y1, p, at(0, 1))
        relay(p - 1)
        if p == 2:
            start_sums()
        if p >= 2:
            multiply(p - 2)
    relay(PARTS - 1)
    multiply(PARTS - 2)
    multiply(PARTS - 1)

    def over_rows(sums, down, across):
        kept = jnp.where(down < across, sums, -1.0)
        return jnp.max(kept.reshape(SLOTS // 8, 8, SLOTS), axis=0)

    def over_columns(sums, down, across):
        return jnp.where(across < down, sums, -1.0)

    across = {b: meta_across(b)[1] for b in (OWN, Y1, Y2)}
    down = {b: meta_down(b)[1] for b in range(BLOCKS)}
    lanes = {b: None for b in range(BLOCKS)}
    rows = {b: None for b in range(BLOCKS)}

    def merge(table, key, value):
        table[key] = value if table[key] is None else jnp.maximum(table[key], value)

    for a in range(2):
        for b in range(2):
            sums = acc_xy[a, b]
            merge(rows, X1 + a, over_columns(sums, down[X1 + a], across[Y1 + b]))
            if (a, b) != (1, 1):
                merge(lanes, Y1 + b, over_rows(sums, down[X1 + a], across[Y1 + b]))
    for block in range(BLOCKS):
        sums = acc_own[block]
        merge(lanes, OWN, over_rows(sums, down[block], across[OWN]))
        if block in (XY, X1, Y1):
            merge(rows, block, over_columns(sums, down[block], across[OWN]))
    for n, block in enumerate((XY, X1, X2, Y1)):
        downs[n, :, :SLOTS] = rows[block]
        narrow = jnp.maximum(downs[n, :, :128], downs[n, :, 128:])
        turned = jnp.max(narrow.T, axis=0, keepdims=True)
        merge(lanes, block, jnp.broadcast_to(turned, (8, SLOTS)))
    for block in range(BLOCKS):
        best[block, :, :SLOTS] = lanes[block]

    p_copies = []
    for n, block in enumerate(RETURNS):
        p_copies.append(push(best.at[block], part.at[n], p_send.at[n], p_recv.at[n], back[block]))
    total = best[OWN]
    for n in range(len(RETURNS)):
        p_copies[n].wait_recv()
        total = jnp.maximum(total, part[n])
    total = jnp.max(total, axis=0, keepdims=True)
    total_ref[...] = jnp.broadcast_to(total, (8, 256))
    a_copies = []
    for k in (4, 3, 5, 2, 6, 1, 7, 0):
        for n, to in ((k, c), (NZ + k, 1 - c)):
            if n:
                a_copies.append(
                    push(total_ref, ans.at[n], a_send.at[n], a_recv.at[n], at_z(-k, to))
                )
    ans[0] = total_ref[...]
    spot = lax.broadcasted_iota(jnp.int32, (SLOTS, DOCS), 0) == slot
    line = 8 * (offset + jnp.where(core == c, 0, NZ))
    here = lax.broadcasted_iota(jnp.int32, (2 * NZ * 8, DOCS), 0) == line
    for copy in a_copies:
        copy.wait_recv()
    values = jnp.dot(
        ans[:, :, :SLOTS].reshape(2 * NZ * 8, SLOTS),
        spot.astype(jnp.float32),
        preferred_element_type=jnp.float32,
        precision=lax.Precision.HIGHEST,
    )
    out_ref[...] = jnp.sum(jnp.where(here, values, 0.0), axis=0, keepdims=True)
    for copy in sent:
        copy.wait_send()


def local(embeddings, cluster_ids, order_index):
    dma = pltpu.SemaphoreType.DMA
    f32, bf16 = jnp.float32, jnp.bfloat16
    result = pl.pallas_call(
        kernel,
        out_shape=jax.ShapeDtypeStruct((1, DOCS), jnp.float32),
        in_specs=[pl.BlockSpec(memory_space=pl.ANY)] * 3,
        out_specs=pl.BlockSpec(memory_space=pltpu.VMEM),
        scratch_shapes=[
            pltpu.VMEM((DOCS, D), bf16),
            pltpu.VMEM((1, DOCS), jnp.int32),
            pltpu.VMEM((1, DOCS), jnp.int32),
            pltpu.VMEM((4, SLOTS, 256), f32),
            pltpu.VMEM((2, 8, 128), f32),
            pltpu.VMEM((BLOCKS, 8, 256), f32),
            pltpu.VMEM((len(RETURNS), 8, 256), f32),
            pltpu.VMEM((8, 256), f32),
            pltpu.VMEM((2 * NZ, 8, 256), f32),
            pltpu.VMEM((BLOCKS, SLOTS, SLOTS), f32),
            pltpu.VMEM((2, 2, SLOTS, SLOTS), f32),
            pltpu.VMEM((2, DOCS, D), bf16),
            pltpu.VMEM((NZ - 1, CHUNK, W), bf16),
            pltpu.VMEM((BLOCKS, NZ, CHUNK, W), bf16),
            dma((3,)),
            dma((2,)),
            dma((2,)),
            dma((PARTS, NZ)),
            dma((PARTS, NZ)),
            dma((BLOCKS, PARTS + 1)),
            dma((BLOCKS, PARTS + 1)),
            dma((len(RETURNS),)),
            dma((len(RETURNS),)),
            dma((2 * NZ,)),
            dma((2 * NZ,)),
            pltpu.SemaphoreType.REGULAR,
            pltpu.SemaphoreType.REGULAR,
        ],
        compiler_params=pltpu.CompilerParams(
            collective_id=0, has_side_effects=True, vmem_limit_bytes=67043328 - 384 * 1024
        ),
    )(embeddings, cluster_ids.reshape(1, DOCS), order_index.reshape(1, DOCS))
    return result.reshape(DOCS)


def solution(mesh):
    placed = (P(("group", "member"), None), P(("group", "member")), P(("group", "member")))
    return jax.shard_map(
        local, mesh=mesh, in_specs=placed, out_specs=P(("group", "member")), check_vma=False
    )
```

```python
import jax
import jax.numpy as jnp
from jax import lax
from jax.experimental import pallas as pl
from jax.experimental.pallas import tpu as pltpu
from jax.sharding import PartitionSpec as P

MESH = pl.DeviceIdType.MESH

NX, NY, NZ = 4, 4, 8
DOCS = 96
CAP = 12
CHUNK = 2 * CAP
SLOTS = NZ * CHUNK
D = 4096
META = 128
W = META + D
WIDTHS = (256,)+(512,) * 7 + (256,)
PARTS = len(WIDTHS)
STARTS = tuple(META + sum(WIDTHS[:p]) for p in range(PARTS))
ENDS = tuple(s + w for s, w in zip(STARTS, WIDTHS))
OFFSETS = (0, 1, 7, 2, 3, 4, 5, 6)
NEAR = 1
AHEAD = 3
FAR = (5, 4, 6, 3, 7, 1, 2)
REST = pl.ds(NEAR, NZ - NEAR)

OWN, XY, X1, X2, Y1, Y2 = range(6)
BLOCKS = 6
RETURNS = (X2, Y2, XY, X1, Y1)


def nt_dot(a, b):
    return lax.dot_general(
        a, b, (((1,), (1,)), ((), ())), preferred_element_type=jnp.float32
    )


def kernel(*refs):
    emb_hbm, ids_hbm, ord_hbm, out_ref, emb, ids_ref, ord_ref = refs[:7]
    downs, mrows, best, part, total_ref, ans, acc_own, acc_xy, units, outb, buf = refs[7:18]
    (
        in_sem, sib_send, sib_recv, z_send, z_recv, send, recv, p_send, p_recv, a_send, a_recv,
        near, far,
    ) = refs[18:]

    gi = lax.axis_index("group")
    mi = lax.axis_index("member")
    x, y = gi // NY, lax.rem(gi, NY)
    z, c = mi // 2, lax.rem(mi, 2)
    sign = 1 - 2 * c

    def at(dx, dy):
        return (
            lax.rem(x + sign * dx + NX, NX) * NY + lax.rem(y + sign * dy + NY, NY),
            mi,
        )

    def at_z(step, core=c):
        return (gi, lax.rem(z + step + NZ, NZ) * 2 + core)

    def bounds(p):
        return (0 if p == 0 else STARTS[p]), ENDS[p]

    def span(p):
        first, last = bounds(p)
        return pl.ds(first, last - first)

    sibling = at_z(0, 1 - c)
    back = {X1: at(-1, 0), Y1: at(0, -1), XY: at(-1, -1), X2: at(-2, 0), Y2: at(0, -2)}

    loads = [
        pltpu.make_async_copy(ids_hbm, ids_ref, in_sem.at[0]),
        pltpu.make_async_copy(ord_hbm, ord_ref, in_sem.at[1]),
        pltpu.make_async_copy(emb_hbm, emb, in_sem.at[2]),
    ]
    for load in loads:
        load.start()

    peers = [sibling, at(1, 0), at(0, 1), at(-1, 0), at(0, -1), at_z(1), at_z(-1)]
    barrier = pltpu.get_barrier_semaphore()
    for peer in peers:
        pl.semaphore_signal(barrier, inc=1, device_id=peer, device_id_type=MESH)

    loads[0].wait()
    loads[1].wait()
    ids = ids_ref[...]
    order = ord_ref[...]
    target = ids // 2
    hit = lax.broadcasted_iota(jnp.int32, (16, DOCS), 0) == target
    hit_f = hit.astype(jnp.float32)
    tri = lax.broadcasted_iota(jnp.int32, (DOCS, DOCS), 0) < lax.broadcasted_iota(
        jnp.int32, (DOCS, DOCS), 1
    )
    count = jnp.dot(
        hit_f.astype(jnp.bfloat16), tri.astype(jnp.bfloat16), preferred_element_type=jnp.float32
    )
    rank = jnp.sum(hit_f * count, axis=0, keepdims=True).astype(jnp.int32)
    offset = lax.rem(target // 2 - z + NZ, NZ)
    core = lax.rem(target, 2)
    inner = c * CAP + rank
    place = jnp.where(offset <= 1, offset, jnp.where(offset == 7, 2, offset + 1))
    slot = place * CHUNK + inner
    to_core0 = jnp.where(core == 0, slot, -1).astype(jnp.float32)
    to_core1 = jnp.where(core == 1, slot, -1).astype(jnp.float32)
    high = order // 256
    low = order - high * 256
    row_id = lax.broadcasted_iota(jnp.int32, (8, DOCS), 0)
    packed = jnp.where(row_id == 0, to_core0, 0.0)
    packed = jnp.where(row_id == 1, to_core1, packed)
    packed = jnp.where(row_id == 2, (ids + 1).astype(jnp.float32), packed)
    packed = jnp.where(row_id == 3, high.astype(jnp.float32), packed)
    packed = jnp.where(row_id == 4, low.astype(jnp.float32), packed)
    mrows[0, :, :DOCS] = packed
    mrows[0, :, DOCS:] = jnp.zeros((8, 128 - DOCS), jnp.float32)

    pl.semaphore_wait(barrier, len(peers))

    for step in (1, -1):
        pl.semaphore_signal(near, inc=1, device_id=at_z(step), device_id_type=MESH)

    sent = []

    def push(src, dst, ssem, rsem, device):
        copy = pltpu.make_async_remote_copy(
            src_ref=src, dst_ref=dst, send_sem=ssem, recv_sem=rsem,
            device_id=device, device_id_type=MESH,
        )
        copy.start()
        sent.append(copy)
        return copy

    meta_copy = push(mrows.at[0], mrows.at[1], sib_send.at[2], sib_recv.at[2], sibling)

    loads[2].wait()
    unit_copies = []
    for half in range(2):

        @pl.loop(half * 3, half * 3 + 3)
        def _(i):
            rows = pl.ds(pl.multiple_of(i * 16, 16), 16)
            values = emb[rows, :].astype(jnp.float32)
            total = jnp.sum(values * values, axis=1, keepdims=True) + D * 1e-06
            units[0, rows, :] = (values * lax.rsqrt(total)).astype(jnp.bfloat16)

        rows = pl.ds(half * 48, 48)
        unit_copies.append(
            push(
                units.at[0, rows], units.at[1, rows],
                sib_send.at[half], sib_recv.at[half], sibling,
            )
        )

    slot_iota = lax.broadcasted_iota(jnp.int32, (SLOTS, DOCS), 0).astype(jnp.float32)

    def table_of(which):
        rows = mrows[which]
        mine = jnp.where(c == 0, rows[0:1, :DOCS], rows[1:2, :DOCS])
        table = (slot_iota == mine).astype(jnp.bfloat16)
        lanes = lax.broadcasted_iota(jnp.int32, (META, DOCS), 0)
        cols = jnp.where(lanes == 0, rows[2:3, :DOCS], 0.0)
        cols = jnp.where(lanes == 1, rows[3:4, :DOCS], cols)
        cols = jnp.where(lanes == 2, rows[4:5, :DOCS], cols)
        return table, nt_dot(table, cols.astype(jnp.bfloat16))

    table_a, meta_a = table_of(0)
    meta_copy.wait_recv()
    table_b, meta_b = table_of(1)

    pl.semaphore_wait(near, 2)
    for step in (2, -2):
        pl.semaphore_signal(far, inc=1, device_id=at_z(step), device_id_type=MESH)

    copies = {}

    def forward(src, dst, q, device, half=None):
        first, last = (0, W) if q < NEAR else bounds(q - NEAR)
        middle = first + (last - first) // 256 * 128
        if half is not None:
            first, last = ((first, middle), (middle, last))[half]
        chunks = pl.ds(q, 1) if q < NEAR else REST
        piece = lambda block: buf.at[block, chunks, :, pl.ds(first, last - first)]
        slot = (dst, q) if half != 1 else (BLOCKS, q)
        copies[(dst, q, half)] = push(
            piece(src), piece(dst), send.at[slot], recv.at[slot], device
        )

    def pass_on(q):
        forward(OWN, X1, q, at(1, 0))
        forward(OWN, Y1, q, at(0, 1))

    done = set()

    def arrived(block, q):
        if (block, q) not in done:
            done.add((block, q))
            for half in (0, 1) if block == XY else (None,):
                copies[(block, q, half)].wait_recv()

    def relay(q):
        arrived(X1, q)
        forward(X1, X2, q, at(1, 0))
        forward(X1, XY, q, at(0, 1), 0)
        arrived(Y1, q)
        forward(Y1, Y2, q, at(0, 1))
        forward(Y1, XY, q, at(1, 0), 1)

    def build(first, last, start, end):
        columns = pl.ds(start - META, end - start)
        rows = jnp.dot(
            table_a[first * CHUNK : last * CHUNK], units[0, :, columns],
            preferred_element_type=jnp.float32,
        )
        rows += jnp.dot(
            table_b[first * CHUNK : last * CHUNK], units[1, :, columns],
            preferred_element_type=jnp.float32,
        )
        rows = rows.reshape(last - first, CHUNK, end - start).astype(jnp.bfloat16)
        if first:
            outb[first - 1 : last - 1, :, start:end] = rows
        else:
            buf[OWN, 0, :, start:end] = rows[0]

    for copy in unit_copies:
        copy.wait_recv()
    meta = (meta_a + meta_b).reshape(NZ, CHUNK, META).astype(jnp.bfloat16)
    buf[OWN, 0, :, :META] = meta[0]
    outb[:, :, :META] = meta[1:]
    for start in range(META, W, 1024):
        build(0, 1, start, start + 1024)
    pass_on(0)
    z_copies = {}
    def send_far(p):
        if p < PARTS:
            columns = span(p)
            for k in FAR:
                z_copies[p, k] = push(
                    outb.at[k - 1, :, columns], buf.at[OWN, k, :, columns],
                    z_send.at[p, k], z_recv.at[p, k], at_z(OFFSETS[k]),
                )

    for p in range(PARTS):
        build(NEAR, NZ, STARTS[p], ENDS[p])
        if p == 0:
            pl.semaphore_wait(far, 2)
        if p < AHEAD:
            send_far(p)

    def multiply(p):
        for block in (XY, X2, Y2):
            arrived(block, p + NEAR)
        columns = pl.ds(STARTS[p], WIDTHS[p])

        def rows_of(block):
            return buf[block, :, :, columns].reshape(SLOTS, WIDTHS[p])

        rows = rows_of(OWN)
        for block in range(BLOCKS):
            acc_own[block] += nt_dot(rows_of(block), rows)
        for b in range(2):
            rows = rows_of(Y1 + b)
            for a in range(2):
                acc_xy[a, b] += nt_dot(rows_of(X1 + a), rows)

    pick_row = lax.broadcasted_iota(jnp.int32, (8, META), 0)
    pick_lane = lax.broadcasted_iota(jnp.int32, (8, META), 1)
    pick = jnp.where((pick_row == 0) & (pick_lane == 0), 1.0, 0.0)
    pick = jnp.where((pick_row == 1) & (pick_lane == 1), 256.0, pick)
    pick = jnp.where((pick_row == 1) & (pick_lane == 2), 1.0, pick).astype(jnp.bfloat16)

    def meta_of(block):
        return buf[block, :, :, :META].reshape(SLOTS, META)

    def meta_down(block):
        values = meta_of(block).astype(jnp.float32)
        return values[:, 0:1], values[:, 1:2] * 256.0 + values[:, 2:3]

    def meta_across(block):
        values = nt_dot(pick, meta_of(block))
        return values[0:1, :], values[1:2, :]

    def start_sums():
        for block in (XY, X2, Y2):
            for q in range(NEAR + 1):
                arrived(block, q)
        across = {b: meta_across(b)[0] for b in (OWN, Y1, Y2)}
        for block in range(BLOCKS):
            down = meta_down(block)[0]
            acc_own[block] = jnp.where(down == across[OWN], 0.0, -4.0)
            if block in (X1, X2):
                for b in range(2):
                    acc_xy[block - X1, b] = jnp.where(down == across[Y1 + b], 0.0, -4.0)
        downs[...] = jnp.full(downs.shape, -1.0, jnp.float32)

    relay(0)
    for p in range(PARTS):
        for k in FAR:
            z_copies[p, k].wait_recv()
        send_far(p + AHEAD)
        pass_on(p + NEAR)
        if p:
            relay(p)
        if p == 2:
            start_sums()
        if p >= 2:
            multiply(p - 2)
    relay(PARTS + NEAR - 1)
    multiply(PARTS - 2)
    multiply(PARTS - 1)

    def over_rows(sums, down, across):
        kept = jnp.where(down < across, sums, -1.0)
        return jnp.max(kept.reshape(SLOTS // 8, 8, SLOTS), axis=0)

    def over_columns(sums, down, across):
        return jnp.where(across < down, sums, -1.0)

    across = {b: meta_across(b)[1] for b in (OWN, Y1, Y2)}
    down = {b: meta_down(b)[1] for b in range(BLOCKS)}
    lanes = {b: None for b in range(BLOCKS)}
    rows = {b: None for b in range(BLOCKS)}

    def merge(table, key, value):
        table[key] = value if table[key] is None else jnp.maximum(table[key], value)

    for a in range(2):
        for b in range(2):
            sums = acc_xy[a, b]
            merge(rows, X1 + a, over_columns(sums, down[X1 + a], across[Y1 + b]))
            if (a, b) != (1, 1):
                merge(lanes, Y1 + b, over_rows(sums, down[X1 + a], across[Y1 + b]))
    for block in (XY, X1, Y1):
        merge(rows, block, over_columns(acc_own[block], down[block], across[OWN]))
    p_copies = []
    for n, block in enumerate(RETURNS):
        if block in rows and rows[block] is not None:
            downs[n, :, :SLOTS] = rows[block]
            narrow = jnp.maximum(downs[n, :, :128], downs[n, :, 128:])
            turned = jnp.max(narrow.T, axis=0, keepdims=True)
            merge(lanes, block, jnp.broadcast_to(turned, (8, SLOTS)))
        best[block, :, :SLOTS] = jnp.max(lanes[block], axis=0, keepdims=True)
        p_copies.append(push(best.at[block], part.at[n], p_send.at[n], p_recv.at[n], back[block]))
    for block in range(BLOCKS):
        merge(lanes, OWN, over_rows(acc_own[block], down[block], across[OWN]))
    best[OWN, :, :SLOTS] = jnp.max(lanes[OWN], axis=0, keepdims=True)
    total = best[OWN]
    for n in range(len(RETURNS)):
        p_copies[n].wait_recv()
        total = jnp.maximum(total, part[n])
    total_ref[...] = total
    a_copies = []
    for k in FAR + (0,):
        for n, to in ((k, c), (NZ + k, 1 - c)):
            if n:
                a_copies.append(
                    push(total_ref, ans.at[n], a_send.at[n], a_recv.at[n], at_z(-OFFSETS[k], to))
                )
    ans[0] = total_ref[...]
    spot = lax.broadcasted_iota(jnp.int32, (SLOTS, DOCS), 0) == slot
    line = place + jnp.where(core == c, 0, NZ)
    here = lax.broadcasted_iota(jnp.int32, (2 * NZ, DOCS), 0) == line
    for copy in a_copies:
        copy.wait_recv()
    values = jnp.dot(
        ans[:, :, :SLOTS].reshape(2 * NZ, SLOTS),
        spot.astype(jnp.float32),
        preferred_element_type=jnp.float32,
        precision=lax.Precision.HIGHEST,
    )
    out_ref[...] = jnp.sum(jnp.where(here, values, 0.0), axis=0, keepdims=True)
    for copy in sent:
        copy.wait_send()


def local(embeddings, cluster_ids, order_index):
    dma = pltpu.SemaphoreType.DMA
    f32, bf16 = jnp.float32, jnp.bfloat16
    result = pl.pallas_call(
        kernel,
        out_shape=jax.ShapeDtypeStruct((1, DOCS), jnp.float32),
        in_specs=[pl.BlockSpec(memory_space=pl.ANY)] * 3,
        out_specs=pl.BlockSpec(memory_space=pltpu.VMEM),
        scratch_shapes=[
            pltpu.VMEM((DOCS, D), bf16),
            pltpu.VMEM((1, DOCS), jnp.int32),
            pltpu.VMEM((1, DOCS), jnp.int32),
            pltpu.VMEM((len(RETURNS), SLOTS, 256), f32),
            pltpu.VMEM((2, 8, 128), f32),
            pltpu.VMEM((BLOCKS, 1, 256), f32),
            pltpu.VMEM((len(RETURNS), 1, 256), f32),
            pltpu.VMEM((1, 256), f32),
            pltpu.VMEM((2 * NZ, 1, 256), f32),
            pltpu.VMEM((BLOCKS, SLOTS, SLOTS), f32),
            pltpu.VMEM((2, 2, SLOTS, SLOTS), f32),
            pltpu.VMEM((2, DOCS, D), bf16),
            pltpu.VMEM((NZ - 1, CHUNK, W), bf16),
            pltpu.VMEM((BLOCKS, NZ, CHUNK, W), bf16),
            dma((3,)),
            dma((3,)),
            dma((3,)),
            dma((PARTS + 1, NZ)),
            dma((PARTS + 1, NZ)),
            dma((BLOCKS + 1, PARTS + NEAR)),
            dma((BLOCKS + 1, PARTS + NEAR)),
            dma((len(RETURNS),)),
            dma((len(RETURNS),)),
            dma((2 * NZ,)),
            dma((2 * NZ,)),
            pltpu.SemaphoreType.REGULAR,
            pltpu.SemaphoreType.REGULAR,
        ],
        compiler_params=pltpu.CompilerParams(
            collective_id=0, has_side_effects=True, vmem_limit_bytes=67043328 - 384 * 1024
        ),
    )(embeddings, cluster_ids.reshape(1, DOCS), order_index.reshape(1, DOCS))
    return result.reshape(DOCS)


def solution(mesh):
    placed = (P(("group", "member"), None), P(("group", "member")), P(("group", "member")))
    return jax.shard_map(
        local, mesh=mesh, in_specs=placed, out_specs=P(("group", "member")), check_vma=False
    )
```

```python
import jax
import jax.numpy as jnp
from jax import lax
from jax.experimental import pallas as pl
from jax.experimental.pallas import tpu as pltpu
from jax.sharding import PartitionSpec as P

MESH = pl.DeviceIdType.MESH

NX, NY, NZ = 4, 4, 8
DOCS = 96
CAP = 12
CHUNK = 2 * CAP
SLOTS = NZ * CHUNK
D = 4096
META = 128
W = META + D
WIDTHS = (256,)+(512,) * 7 + (256,)
PARTS = len(WIDTHS)
STARTS = tuple(META + sum(WIDTHS[:p]) for p in range(PARTS))
ENDS = tuple(s + w for s, w in zip(STARTS, WIDTHS))
OFFSETS = (0, 1, 7, 2, 3, 4, 5, 6)
NEAR = 1
AHEAD = 3
LAG = 3
FAR = (5, 4, 6, 3, 7, 1, 2)
REST = pl.ds(NEAR, NZ - NEAR)

OWN, XY, X1, X2, Y1, Y2 = range(6)
BLOCKS = 6
RETURNS = (X2, Y2, XY, X1, Y1)


def nt_dot(a, b):
    return lax.dot_general(
        a, b, (((1,), (1,)), ((), ())), preferred_element_type=jnp.float32
    )


def kernel(*refs):
    emb_hbm, ids_hbm, ord_hbm, out_ref, emb, ids_ref, ord_ref = refs[:7]
    downs, mrows, best, part, total_ref, ans, acc_own, acc_xy, units, outb, buf = refs[7:18]
    (
        in_sem, sib_send, sib_recv, z_send, z_recv, send, recv, p_send, p_recv, a_send, a_recv,
        near, far,
    ) = refs[18:]

    gi = lax.axis_index("group")
    mi = lax.axis_index("member")
    x, y = gi // NY, lax.rem(gi, NY)
    z, c = mi // 2, lax.rem(mi, 2)
    sign = 1 - 2 * c

    def at(dx, dy):
        return (
            lax.rem(x + sign * dx + NX, NX) * NY + lax.rem(y + sign * dy + NY, NY),
            mi,
        )

    def at_z(step, core=c):
        return (gi, lax.rem(z + step + NZ, NZ) * 2 + core)

    def bounds(p):
        return (0 if p == 0 else STARTS[p]), ENDS[p]

    def span(p):
        first, last = bounds(p)
        return pl.ds(first, last - first)

    sibling = at_z(0, 1 - c)
    back = {X1: at(-1, 0), Y1: at(0, -1), XY: at(-1, -1), X2: at(-2, 0), Y2: at(0, -2)}

    loads = [
        pltpu.make_async_copy(ids_hbm, ids_ref, in_sem.at[0]),
        pltpu.make_async_copy(ord_hbm, ord_ref, in_sem.at[1]),
        pltpu.make_async_copy(emb_hbm, emb, in_sem.at[2]),
    ]
    for load in loads:
        load.start()

    peers = [sibling, at(1, 0), at(0, 1), at(-1, 0), at(0, -1), at_z(1), at_z(-1)]
    barrier = pltpu.get_barrier_semaphore()
    for peer in peers:
        pl.semaphore_signal(barrier, inc=1, device_id=peer, device_id_type=MESH)

    loads[0].wait()
    loads[1].wait()
    ids = ids_ref[...]
    order = ord_ref[...]
    target = ids // 2
    hit = lax.broadcasted_iota(jnp.int32, (16, DOCS), 0) == target
    hit_f = hit.astype(jnp.float32)
    tri = lax.broadcasted_iota(jnp.int32, (DOCS, DOCS), 0) < lax.broadcasted_iota(
        jnp.int32, (DOCS, DOCS), 1
    )
    count = jnp.dot(
        hit_f.astype(jnp.bfloat16), tri.astype(jnp.bfloat16), preferred_element_type=jnp.float32
    )
    rank = jnp.sum(hit_f * count, axis=0, keepdims=True).astype(jnp.int32)
    offset = lax.rem(target // 2 - z + NZ, NZ)
    core = lax.rem(target, 2)
    inner = c * CAP + rank
    place = jnp.where(offset <= 1, offset, jnp.where(offset == 7, 2, offset + 1))
    slot = place * CHUNK + inner
    to_core0 = jnp.where(core == 0, slot, -1).astype(jnp.float32)
    to_core1 = jnp.where(core == 1, slot, -1).astype(jnp.float32)
    high = order // 256
    low = order - high * 256
    row_id = lax.broadcasted_iota(jnp.int32, (8, DOCS), 0)
    packed = jnp.where(row_id == 0, to_core0, 0.0)
    packed = jnp.where(row_id == 1, to_core1, packed)
    packed = jnp.where(row_id == 2, (ids + 1).astype(jnp.float32), packed)
    packed = jnp.where(row_id == 3, high.astype(jnp.float32), packed)
    packed = jnp.where(row_id == 4, low.astype(jnp.float32), packed)
    mrows[0, :, :DOCS] = packed
    mrows[0, :, DOCS:] = jnp.zeros((8, 128 - DOCS), jnp.float32)

    pl.semaphore_wait(barrier, len(peers))

    for step in (1, -1):
        pl.semaphore_signal(near, inc=1, device_id=at_z(step), device_id_type=MESH)

    sent = []

    def push(src, dst, ssem, rsem, device):
        copy = pltpu.make_async_remote_copy(
            src_ref=src, dst_ref=dst, send_sem=ssem, recv_sem=rsem,
            device_id=device, device_id_type=MESH,
        )
        copy.start()
        sent.append(copy)
        return copy

    meta_copy = push(mrows.at[0], mrows.at[1], sib_send.at[2], sib_recv.at[2], sibling)

    loads[2].wait()
    unit_copies = []
    for half in range(2):

        @pl.loop(half * 3, half * 3 + 3)
        def _(i):
            rows = pl.ds(pl.multiple_of(i * 16, 16), 16)
            values = emb[rows, :].astype(jnp.float32)
            total = jnp.sum(values * values, axis=1, keepdims=True) + D * 1e-06
            units[0, rows, :] = (values * lax.rsqrt(total)).astype(jnp.bfloat16)

        rows = pl.ds(half * 48, 48)
        unit_copies.append(
            push(
                units.at[0, rows], units.at[1, rows],
                sib_send.at[half], sib_recv.at[half], sibling,
            )
        )

    slot_iota = lax.broadcasted_iota(jnp.int32, (SLOTS, DOCS), 0).astype(jnp.float32)

    def table_of(which):
        rows = mrows[which]
        mine = jnp.where(c == 0, rows[0:1, :DOCS], rows[1:2, :DOCS])
        table = (slot_iota == mine).astype(jnp.bfloat16)
        lanes = lax.broadcasted_iota(jnp.int32, (META, DOCS), 0)
        cols = jnp.where(lanes == 0, rows[2:3, :DOCS], 0.0)
        cols = jnp.where(lanes == 1, rows[3:4, :DOCS], cols)
        cols = jnp.where(lanes == 2, rows[4:5, :DOCS], cols)
        return table, nt_dot(table, cols.astype(jnp.bfloat16))

    table_a, meta_a = table_of(0)
    meta_copy.wait_recv()
    table_b, meta_b = table_of(1)

    pl.semaphore_wait(near, 2)
    for step in (2, -2):
        pl.semaphore_signal(far, inc=1, device_id=at_z(step), device_id_type=MESH)

    copies = {}

    def forward(src, dst, q, device, half=None):
        first, last = (0, W) if q < NEAR else bounds(q - NEAR)
        middle = first + (last - first) // 256 * 128
        if half is not None:
            first, last = ((first, middle), (middle, last))[half]
        chunks = pl.ds(q, 1) if q < NEAR else REST
        piece = lambda block: buf.at[block, chunks, :, pl.ds(first, last - first)]
        slot = (dst, q) if half != 1 else (BLOCKS, q)
        copies[(dst, q, half)] = push(
            piece(src), piece(dst), send.at[slot], recv.at[slot], device
        )

    def pass_on(q):
        forward(OWN, X1, q, at(1, 0))
        forward(OWN, Y1, q, at(0, 1))

    done = set()

    def arrived(block, q):
        if (block, q) not in done:
            done.add((block, q))
            for half in (0, 1) if block == XY else (None,):
                copies[(block, q, half)].wait_recv()

    def relay(q):
        arrived(X1, q)
        forward(X1, X2, q, at(1, 0))
        forward(X1, XY, q, at(0, 1), 0)
        arrived(Y1, q)
        forward(Y1, Y2, q, at(0, 1))
        forward(Y1, XY, q, at(1, 0), 1)

    def build(first, last, start, end):
        columns = pl.ds(start - META, end - start)
        rows = jnp.dot(
            table_a[first * CHUNK : last * CHUNK], units[0, :, columns],
            preferred_element_type=jnp.float32,
        )
        rows += jnp.dot(
            table_b[first * CHUNK : last * CHUNK], units[1, :, columns],
            preferred_element_type=jnp.float32,
        )
        rows = rows.reshape(last - first, CHUNK, end - start).astype(jnp.bfloat16)
        if first:
            outb[first - 1 : last - 1, :, start:end] = rows
        else:
            buf[OWN, 0, :, start:end] = rows[0]

    for copy in unit_copies:
        copy.wait_recv()
    meta = (meta_a + meta_b).reshape(NZ, CHUNK, META).astype(jnp.bfloat16)
    buf[OWN, 0, :, :META] = meta[0]
    outb[:, :, :META] = meta[1:]
    for start in range(META, W, 1024):
        build(0, 1, start, start + 1024)
    pass_on(0)
    z_copies = {}
    def send_far(p):
        if p < PARTS:
            columns = span(p)
            for k in FAR:
                z_copies[p, k] = push(
                    outb.at[k - 1, :, columns], buf.at[OWN, k, :, columns],
                    z_send.at[p, k], z_recv.at[p, k], at_z(OFFSETS[k]),
                )

    for p in range(PARTS):
        build(NEAR, NZ, STARTS[p], ENDS[p])
        if p == 0:
            pl.semaphore_wait(far, 2)
        if p < AHEAD:
            send_far(p)

    def multiply(p):
        for block in (XY, X2, Y2):
            arrived(block, p + NEAR)
        columns = pl.ds(STARTS[p], WIDTHS[p])

        def rows_of(block):
            return buf[block, :, :, columns].reshape(SLOTS, WIDTHS[p])

        rows = rows_of(OWN)
        for block in range(BLOCKS):
            acc_own[block] += nt_dot(rows_of(block), rows)
        for b in range(2):
            rows = rows_of(Y1 + b)
            for a in range(2):
                acc_xy[a, b] += nt_dot(rows_of(X1 + a), rows)

    pick_row = lax.broadcasted_iota(jnp.int32, (8, META), 0)
    pick_lane = lax.broadcasted_iota(jnp.int32, (8, META), 1)
    pick = jnp.where((pick_row == 0) & (pick_lane == 0), 1.0, 0.0)
    pick = jnp.where((pick_row == 1) & (pick_lane == 1), 256.0, pick)
    pick = jnp.where((pick_row == 1) & (pick_lane == 2), 1.0, pick).astype(jnp.bfloat16)

    def meta_of(block):
        return buf[block, :, :, :META].reshape(SLOTS, META)

    def meta_down(block):
        values = meta_of(block).astype(jnp.float32)
        return values[:, 0:1], values[:, 1:2] * 256.0 + values[:, 2:3]

    def meta_across(block):
        values = nt_dot(pick, meta_of(block))
        return values[0:1, :], values[1:2, :]

    def start_sums():
        for block in (XY, X2, Y2):
            for q in range(NEAR + 1):
                arrived(block, q)
        across = {b: meta_across(b)[0] for b in (OWN, Y1, Y2)}
        for block in range(BLOCKS):
            down = meta_down(block)[0]
            acc_own[block] = jnp.where(down == across[OWN], 0.0, -4.0)
            if block in (X1, X2):
                for b in range(2):
                    acc_xy[block - X1, b] = jnp.where(down == across[Y1 + b], 0.0, -4.0)
        downs[...] = jnp.full(downs.shape, -1.0, jnp.float32)

    relay(0)
    for p in range(PARTS):
        for k in FAR:
            z_copies[p, k].wait_recv()
        pass_on(p + NEAR)
        if p:
            relay(p)
        send_far(p + AHEAD)
        if p == LAG:
            start_sums()
        if p >= LAG:
            multiply(p - LAG)
    relay(PARTS + NEAR - 1)
    for p in range(PARTS - LAG, PARTS):
        multiply(p)

    def over_rows(sums, down, across):
        kept = jnp.where(down < across, sums, -1.0)
        return jnp.max(kept.reshape(SLOTS // 8, 8, SLOTS), axis=0)

    def over_columns(sums, down, across):
        return jnp.where(across < down, sums, -1.0)

    across = {b: meta_across(b)[1] for b in (OWN, Y1, Y2)}
    down = {b: meta_down(b)[1] for b in range(BLOCKS)}
    lanes = {b: None for b in range(BLOCKS)}
    rows = {b: None for b in range(BLOCKS)}

    def merge(table, key, value):
        table[key] = value if table[key] is None else jnp.maximum(table[key], value)

    for a in range(2):
        for b in range(2):
            sums = acc_xy[a, b]
            merge(rows, X1 + a, over_columns(sums, down[X1 + a], across[Y1 + b]))
            if (a, b) != (1, 1):
                merge(lanes, Y1 + b, over_rows(sums, down[X1 + a], across[Y1 + b]))
    for block in (XY, X1, Y1):
        merge(rows, block, over_columns(acc_own[block], down[block], across[OWN]))
    p_copies = []
    for n, block in enumerate(RETURNS):
        if block in rows and rows[block] is not None:
            downs[n, :, :SLOTS] = rows[block]
            narrow = jnp.maximum(downs[n, :, :128], downs[n, :, 128:])
            turned = jnp.max(narrow.T, axis=0, keepdims=True)
            merge(lanes, block, jnp.broadcast_to(turned, (8, SLOTS)))
        best[block, :, :SLOTS] = jnp.max(lanes[block], axis=0, keepdims=True)
        p_copies.append(push(best.at[block], part.at[n], p_send.at[n], p_recv.at[n], back[block]))
    for block in range(BLOCKS):
        merge(lanes, OWN, over_rows(acc_own[block], down[block], across[OWN]))
    best[OWN, :, :SLOTS] = jnp.max(lanes[OWN], axis=0, keepdims=True)
    total = best[OWN]
    for n in range(len(RETURNS)):
        p_copies[n].wait_recv()
        total = jnp.maximum(total, part[n])
    total_ref[...] = total
    a_copies = []
    for k in FAR + (0,):
        for n, to in ((k, c), (NZ + k, 1 - c)):
            if n:
                a_copies.append(
                    push(total_ref, ans.at[n], a_send.at[n], a_recv.at[n], at_z(-OFFSETS[k], to))
                )
    ans[0] = total_ref[...]
    spot = lax.broadcasted_iota(jnp.int32, (SLOTS, DOCS), 0) == slot
    line = place + jnp.where(core == c, 0, NZ)
    here = lax.broadcasted_iota(jnp.int32, (2 * NZ, DOCS), 0) == line
    for copy in a_copies:
        copy.wait_recv()
    values = jnp.dot(
        ans[:, :, :SLOTS].reshape(2 * NZ, SLOTS),
        spot.astype(jnp.float32),
        preferred_element_type=jnp.float32,
        precision=lax.Precision.HIGHEST,
    )
    out_ref[...] = jnp.sum(jnp.where(here, values, 0.0), axis=0, keepdims=True)
    for copy in sent:
        copy.wait_send()


def local(embeddings, cluster_ids, order_index):
    dma = pltpu.SemaphoreType.DMA
    f32, bf16 = jnp.float32, jnp.bfloat16
    result = pl.pallas_call(
        kernel,
        out_shape=jax.ShapeDtypeStruct((1, DOCS), jnp.float32),
        in_specs=[pl.BlockSpec(memory_space=pl.ANY)] * 3,
        out_specs=pl.BlockSpec(memory_space=pltpu.VMEM),
        scratch_shapes=[
            pltpu.VMEM((DOCS, D), bf16),
            pltpu.VMEM((1, DOCS), jnp.int32),
            pltpu.VMEM((1, DOCS), jnp.int32),
            pltpu.VMEM((len(RETURNS), SLOTS, 256), f32),
            pltpu.VMEM((2, 8, 128), f32),
            pltpu.VMEM((BLOCKS, 1, 256), f32),
            pltpu.VMEM((len(RETURNS), 1, 256), f32),
            pltpu.VMEM((1, 256), f32),
            pltpu.VMEM((2 * NZ, 1, 256), f32),
            pltpu.VMEM((BLOCKS, SLOTS, SLOTS), f32),
            pltpu.VMEM((2, 2, SLOTS, SLOTS), f32),
            pltpu.VMEM((2, DOCS, D), bf16),
            pltpu.VMEM((NZ - 1, CHUNK, W), bf16),
            pltpu.VMEM((BLOCKS, NZ, CHUNK, W), bf16),
            dma((3,)),
            dma((3,)),
            dma((3,)),
            dma((PARTS + 1, NZ)),
            dma((PARTS + 1, NZ)),
            dma((BLOCKS + 1, PARTS + NEAR)),
            dma((BLOCKS + 1, PARTS + NEAR)),
            dma((len(RETURNS),)),
            dma((len(RETURNS),)),
            dma((2 * NZ,)),
            dma((2 * NZ,)),
            pltpu.SemaphoreType.REGULAR,
            pltpu.SemaphoreType.REGULAR,
        ],
        compiler_params=pltpu.CompilerParams(
            collective_id=0, has_side_effects=True, vmem_limit_bytes=67043328 - 384 * 1024
        ),
    )(embeddings, cluster_ids.reshape(1, DOCS), order_index.reshape(1, DOCS))
    return result.reshape(DOCS)


def solution(mesh):
    placed = (P(("group", "member"), None), P(("group", "member")), P(("group", "member")))
    return jax.shard_map(
        local, mesh=mesh, in_specs=placed, out_specs=P(("group", "member")), check_vma=False
    )
```

```python
import jax
import jax.numpy as jnp
from jax import lax
from jax.experimental import pallas as pl
from jax.experimental.pallas import tpu as pltpu
from jax.sharding import PartitionSpec as P

MESH = pl.DeviceIdType.MESH

NX, NY, NZ = 4, 4, 8
DOCS = 96
CAP = 12
CHUNK = 2 * CAP
SLOTS = NZ * CHUNK
D = 4096
META = 128
W = META + D
WIDTHS = (128, 384) + (512,) * 7
PARTS = len(WIDTHS)
STARTS = tuple(META + sum(WIDTHS[:p]) for p in range(PARTS))
ENDS = tuple(s + w for s, w in zip(STARTS, WIDTHS))
OFFSETS = (0, 1, 7, 2, 3, 4, 5, 6)
NEAR = 1
AHEAD = 3
LAG = 3
FAR = (5, 4, 6, 3, 7, 1, 2)
REST = pl.ds(NEAR, NZ - NEAR)

OWN, XY, X1, X2, Y1, Y2 = range(6)
BLOCKS = 6
RETURNS = (X2, Y2, XY, X1, Y1)


def nt_dot(a, b):
    return lax.dot_general(
        a, b, (((1,), (1,)), ((), ())), preferred_element_type=jnp.float32
    )


def kernel(*refs):
    emb_hbm, ids_hbm, ord_hbm, out_ref, emb, ids_ref, ord_ref = refs[:7]
    downs, mrows, best, part, total_ref, ans, acc_own, acc_xy, units, outb, buf = refs[7:18]
    (
        in_sem, sib_send, sib_recv, z_send, z_recv, send, recv, p_send, p_recv, a_send, a_recv,
        near, far,
    ) = refs[18:]

    gi = lax.axis_index("group")
    mi = lax.axis_index("member")
    x, y = gi // NY, lax.rem(gi, NY)
    z, c = mi // 2, lax.rem(mi, 2)
    sign = 1 - 2 * c

    def at(dx, dy):
        return (
            lax.rem(x + sign * dx + NX, NX) * NY + lax.rem(y + sign * dy + NY, NY),
            mi,
        )

    def at_z(step, core=c):
        return (gi, lax.rem(z + step + NZ, NZ) * 2 + core)

    def bounds(p):
        return (0 if p == 0 else STARTS[p]), ENDS[p]

    def span(p):
        first, last = bounds(p)
        return pl.ds(first, last - first)

    sibling = at_z(0, 1 - c)
    back = {X1: at(-1, 0), Y1: at(0, -1), XY: at(-1, -1), X2: at(-2, 0), Y2: at(0, -2)}

    loads = [
        pltpu.make_async_copy(ids_hbm, ids_ref, in_sem.at[0]),
        pltpu.make_async_copy(ord_hbm, ord_ref, in_sem.at[1]),
        pltpu.make_async_copy(emb_hbm, emb, in_sem.at[2]),
    ]
    for load in loads:
        load.start()

    peers = [sibling, at(1, 0), at(0, 1), at(-1, 0), at(0, -1), at_z(1), at_z(-1)]
    barrier = pltpu.get_barrier_semaphore()
    for peer in peers:
        pl.semaphore_signal(barrier, inc=1, device_id=peer, device_id_type=MESH)

    loads[0].wait()
    loads[1].wait()
    ids = ids_ref[...]
    order = ord_ref[...]
    target = ids // 2
    hit = lax.broadcasted_iota(jnp.int32, (16, DOCS), 0) == target
    hit_f = hit.astype(jnp.float32)
    tri = lax.broadcasted_iota(jnp.int32, (DOCS, DOCS), 0) < lax.broadcasted_iota(
        jnp.int32, (DOCS, DOCS), 1
    )
    count = jnp.dot(
        hit_f.astype(jnp.bfloat16), tri.astype(jnp.bfloat16), preferred_element_type=jnp.float32
    )
    rank = jnp.sum(hit_f * count, axis=0, keepdims=True).astype(jnp.int32)
    offset = lax.rem(target // 2 - z + NZ, NZ)
    core = lax.rem(target, 2)
    inner = c * CAP + rank
    place = jnp.where(offset <= 1, offset, jnp.where(offset == 7, 2, offset + 1))
    slot = place * CHUNK + inner
    to_core0 = jnp.where(core == 0, slot, -1).astype(jnp.float32)
    to_core1 = jnp.where(core == 1, slot, -1).astype(jnp.float32)
    high = order // 256
    low = order - high * 256
    row_id = lax.broadcasted_iota(jnp.int32, (8, DOCS), 0)
    packed = jnp.where(row_id == 0, to_core0, 0.0)
    packed = jnp.where(row_id == 1, to_core1, packed)
    packed = jnp.where(row_id == 2, (ids + 1).astype(jnp.float32), packed)
    packed = jnp.where(row_id == 3, high.astype(jnp.float32), packed)
    packed = jnp.where(row_id == 4, low.astype(jnp.float32), packed)
    mrows[0, :, :DOCS] = packed
    mrows[0, :, DOCS:] = jnp.zeros((8, 128 - DOCS), jnp.float32)

    pl.semaphore_wait(barrier, len(peers))

    for step in (1, -1):
        pl.semaphore_signal(near, inc=1, device_id=at_z(step), device_id_type=MESH)

    sent = []

    def push(src, dst, ssem, rsem, device):
        copy = pltpu.make_async_remote_copy(
            src_ref=src, dst_ref=dst, send_sem=ssem, recv_sem=rsem,
            device_id=device, device_id_type=MESH,
        )
        copy.start()
        sent.append(copy)
        return copy

    meta_copy = push(mrows.at[0], mrows.at[1], sib_send.at[2], sib_recv.at[2], sibling)

    loads[2].wait()
    unit_copies = []
    for half in range(2):

        @pl.loop(half * 3, half * 3 + 3)
        def _(i):
            rows = pl.ds(pl.multiple_of(i * 16, 16), 16)
            values = emb[rows, :].astype(jnp.float32)
            total = jnp.sum(values * values, axis=1, keepdims=True) + D * 1e-06
            units[0, rows, :] = (values * lax.rsqrt(total)).astype(jnp.bfloat16)

        rows = pl.ds(half * 48, 48)
        unit_copies.append(
            push(
                units.at[0, rows], units.at[1, rows],
                sib_send.at[half], sib_recv.at[half], sibling,
            )
        )

    slot_iota = lax.broadcasted_iota(jnp.int32, (SLOTS, DOCS), 0).astype(jnp.float32)

    def table_of(which):
        rows = mrows[which]
        mine = jnp.where(c == 0, rows[0:1, :DOCS], rows[1:2, :DOCS])
        table = (slot_iota == mine).astype(jnp.bfloat16)
        lanes = lax.broadcasted_iota(jnp.int32, (META, DOCS), 0)
        cols = jnp.where(lanes == 0, rows[2:3, :DOCS], 0.0)
        cols = jnp.where(lanes == 1, rows[3:4, :DOCS], cols)
        cols = jnp.where(lanes == 2, rows[4:5, :DOCS], cols)
        return table, nt_dot(table, cols.astype(jnp.bfloat16))

    table_a, meta_a = table_of(0)
    meta_copy.wait_recv()
    table_b, meta_b = table_of(1)

    pl.semaphore_wait(near, 2)
    for step in (2, -2):
        pl.semaphore_signal(far, inc=1, device_id=at_z(step), device_id_type=MESH)

    copies = {}

    def forward(src, dst, q, device, half=None):
        first, last = (0, W) if q < NEAR else bounds(q - NEAR)
        middle = first + (last - first) // 256 * 128
        if half is not None:
            first, last = ((first, middle), (middle, last))[half]
        chunks = pl.ds(q, 1) if q < NEAR else REST
        piece = lambda block: buf.at[block, chunks, :, pl.ds(first, last - first)]
        slot = (dst, q) if half != 1 else (BLOCKS, q)
        copies[(dst, q, half)] = push(
            piece(src), piece(dst), send.at[slot], recv.at[slot], device
        )

    def pass_on(q):
        forward(OWN, X1, q, at(1, 0))
        forward(OWN, Y1, q, at(0, 1))

    done = set()

    def arrived(block, q):
        if (block, q) not in done:
            done.add((block, q))
            for half in (0, 1) if block == XY else (None,):
                copies[(block, q, half)].wait_recv()

    def relay(q):
        arrived(X1, q)
        forward(X1, X2, q, at(1, 0))
        forward(X1, XY, q, at(0, 1), 0)
        arrived(Y1, q)
        forward(Y1, Y2, q, at(0, 1))
        forward(Y1, XY, q, at(1, 0), 1)

    def build(first, last, start, end):
        columns = pl.ds(start - META, end - start)
        rows = jnp.dot(
            table_a[first * CHUNK : last * CHUNK], units[0, :, columns],
            preferred_element_type=jnp.float32,
        )
        rows += jnp.dot(
            table_b[first * CHUNK : last * CHUNK], units[1, :, columns],
            preferred_element_type=jnp.float32,
        )
        rows = rows.reshape(last - first, CHUNK, end - start).astype(jnp.bfloat16)
        if first:
            outb[first - 1 : last - 1, :, start:end] = rows
        else:
            buf[OWN, 0, :, start:end] = rows[0]

    for copy in unit_copies:
        copy.wait_recv()
    meta = (meta_a + meta_b).reshape(NZ, CHUNK, META).astype(jnp.bfloat16)
    buf[OWN, 0, :, :META] = meta[0]
    outb[:, :, :META] = meta[1:]
    for start in range(META, W, 1024):
        build(0, 1, start, start + 1024)
    pass_on(0)
    z_copies = {}
    def send_far(p):
        if p < PARTS:
            columns = span(p)
            for k in FAR:
                z_copies[p, k] = push(
                    outb.at[k - 1, :, columns], buf.at[OWN, k, :, columns],
                    z_send.at[p, k], z_recv.at[p, k], at_z(OFFSETS[k]),
                )

    for p in range(PARTS):
        build(NEAR, NZ, STARTS[p], ENDS[p])
        if p == 0:
            pl.semaphore_wait(far, 2)
        if p < AHEAD:
            send_far(p)

    def multiply(p):
        for block in (XY, X2, Y2):
            arrived(block, p + NEAR)
        columns = pl.ds(STARTS[p], WIDTHS[p])

        def rows_of(block):
            return buf[block, :, :, columns].reshape(SLOTS, WIDTHS[p])

        rows = rows_of(OWN)
        for block in range(BLOCKS):
            acc_own[block] += nt_dot(rows_of(block), rows)
        for b in range(2):
            rows = rows_of(Y1 + b)
            for a in range(2):
                acc_xy[a, b] += nt_dot(rows_of(X1 + a), rows)

    pick_row = lax.broadcasted_iota(jnp.int32, (8, META), 0)
    pick_lane = lax.broadcasted_iota(jnp.int32, (8, META), 1)
    pick = jnp.where((pick_row == 0) & (pick_lane == 0), 1.0, 0.0)
    pick = jnp.where((pick_row == 1) & (pick_lane == 1), 256.0, pick)
    pick = jnp.where((pick_row == 1) & (pick_lane == 2), 1.0, pick).astype(jnp.bfloat16)

    def meta_of(block):
        return buf[block, :, :, :META].reshape(SLOTS, META)

    def meta_down(block):
        values = meta_of(block).astype(jnp.float32)
        return values[:, 0:1], values[:, 1:2] * 256.0 + values[:, 2:3]

    def meta_across(block):
        values = nt_dot(pick, meta_of(block))
        return values[0:1, :], values[1:2, :]

    def start_sums():
        for block in (XY, X2, Y2):
            for q in range(NEAR + 1):
                arrived(block, q)
        across = {b: meta_across(b)[0] for b in (OWN, Y1, Y2)}
        for block in range(BLOCKS):
            down = meta_down(block)[0]
            acc_own[block] = jnp.where(down == across[OWN], 0.0, -4.0)
            if block in (X1, X2):
                for b in range(2):
                    acc_xy[block - X1, b] = jnp.where(down == across[Y1 + b], 0.0, -4.0)
        downs[...] = jnp.full(downs.shape, -1.0, jnp.float32)

    relay(0)
    for p in range(PARTS):
        for k in FAR:
            z_copies[p, k].wait_recv()
        pass_on(p + NEAR)
        if p:
            relay(p)
        send_far(p + AHEAD)
        if p == LAG:
            start_sums()
        if p >= LAG:
            multiply(p - LAG)
    relay(PARTS + NEAR - 1)
    for p in range(PARTS - LAG, PARTS):
        multiply(p)

    def over_rows(sums, down, across):
        kept = jnp.where(down < across, sums, -1.0)
        return jnp.max(kept.reshape(SLOTS // 8, 8, SLOTS), axis=0)

    def over_columns(sums, down, across):
        return jnp.where(across < down, sums, -1.0)

    across = {b: meta_across(b)[1] for b in (OWN, Y1, Y2)}
    down = {b: meta_down(b)[1] for b in range(BLOCKS)}
    lanes = {b: None for b in range(BLOCKS)}
    rows = {b: None for b in range(BLOCKS)}

    def merge(table, key, value):
        table[key] = value if table[key] is None else jnp.maximum(table[key], value)

    for a in range(2):
        for b in range(2):
            sums = acc_xy[a, b]
            merge(rows, X1 + a, over_columns(sums, down[X1 + a], across[Y1 + b]))
            if (a, b) != (1, 1):
                merge(lanes, Y1 + b, over_rows(sums, down[X1 + a], across[Y1 + b]))
    for block in (XY, X1, Y1):
        merge(rows, block, over_columns(acc_own[block], down[block], across[OWN]))
    p_copies = []
    for n, block in enumerate(RETURNS):
        if block in rows and rows[block] is not None:
            downs[n, :, :SLOTS] = rows[block]
            narrow = jnp.maximum(downs[n, :, :128], downs[n, :, 128:])
            turned = jnp.max(narrow.T, axis=0, keepdims=True)
            merge(lanes, block, jnp.broadcast_to(turned, (8, SLOTS)))
        best[block, :, :SLOTS] = jnp.max(lanes[block], axis=0, keepdims=True)
        p_copies.append(push(best.at[block], part.at[n], p_send.at[n], p_recv.at[n], back[block]))
    for block in range(BLOCKS):
        merge(lanes, OWN, over_rows(acc_own[block], down[block], across[OWN]))
    best[OWN, :, :SLOTS] = jnp.max(lanes[OWN], axis=0, keepdims=True)
    total = best[OWN]
    for n in range(len(RETURNS)):
        p_copies[n].wait_recv()
        total = jnp.maximum(total, part[n])
    total_ref[...] = total
    a_copies = []
    for k in FAR + (0,):
        for n, to in ((k, c), (NZ + k, 1 - c)):
            if n:
                a_copies.append(
                    push(total_ref, ans.at[n], a_send.at[n], a_recv.at[n], at_z(-OFFSETS[k], to))
                )
    ans[0] = total_ref[...]
    spot = lax.broadcasted_iota(jnp.int32, (SLOTS, DOCS), 0) == slot
    line = place + jnp.where(core == c, 0, NZ)
    here = lax.broadcasted_iota(jnp.int32, (2 * NZ, DOCS), 0) == line
    for copy in a_copies:
        copy.wait_recv()
    values = jnp.dot(
        ans[:, :, :SLOTS].reshape(2 * NZ, SLOTS),
        spot.astype(jnp.float32),
        preferred_element_type=jnp.float32,
        precision=lax.Precision.HIGHEST,
    )
    out_ref[...] = jnp.sum(jnp.where(here, values, 0.0), axis=0, keepdims=True)
    for copy in sent:
        copy.wait_send()


def local(embeddings, cluster_ids, order_index):
    dma = pltpu.SemaphoreType.DMA
    f32, bf16 = jnp.float32, jnp.bfloat16
    result = pl.pallas_call(
        kernel,
        out_shape=jax.ShapeDtypeStruct((1, DOCS), jnp.float32),
        in_specs=[pl.BlockSpec(memory_space=pl.ANY)] * 3,
        out_specs=pl.BlockSpec(memory_space=pltpu.VMEM),
        scratch_shapes=[
            pltpu.VMEM((DOCS, D), bf16),
            pltpu.VMEM((1, DOCS), jnp.int32),
            pltpu.VMEM((1, DOCS), jnp.int32),
            pltpu.VMEM((len(RETURNS), SLOTS, 256), f32),
            pltpu.VMEM((2, 8, 128), f32),
            pltpu.VMEM((BLOCKS, 1, 256), f32),
            pltpu.VMEM((len(RETURNS), 1, 256), f32),
            pltpu.VMEM((1, 256), f32),
            pltpu.VMEM((2 * NZ, 1, 256), f32),
            pltpu.VMEM((BLOCKS, SLOTS, SLOTS), f32),
            pltpu.VMEM((2, 2, SLOTS, SLOTS), f32),
            pltpu.VMEM((2, DOCS, D), bf16),
            pltpu.VMEM((NZ - 1, CHUNK, W), bf16),
            pltpu.VMEM((BLOCKS, NZ, CHUNK, W), bf16),
            dma((3,)),
            dma((3,)),
            dma((3,)),
            dma((PARTS + 1, NZ)),
            dma((PARTS + 1, NZ)),
            dma((BLOCKS + 1, PARTS + NEAR)),
            dma((BLOCKS + 1, PARTS + NEAR)),
            dma((len(RETURNS),)),
            dma((len(RETURNS),)),
            dma((2 * NZ,)),
            dma((2 * NZ,)),
            pltpu.SemaphoreType.REGULAR,
            pltpu.SemaphoreType.REGULAR,
        ],
        compiler_params=pltpu.CompilerParams(
            collective_id=0, has_side_effects=True, vmem_limit_bytes=67043328 - 384 * 1024
        ),
    )(embeddings, cluster_ids.reshape(1, DOCS), order_index.reshape(1, DOCS))
    return result.reshape(DOCS)


def solution(mesh):
    placed = (P(("group", "member"), None), P(("group", "member")), P(("group", "member")))
    return jax.shard_map(
        local, mesh=mesh, in_specs=placed, out_specs=P(("group", "member")), check_vma=False
    )
```
